32 devices in a mesh: groups: 2 (over x), samp: 8 (over z, y), line: 2 (over core).
Axes of the slice: x: 2, y: 2, z: 4, core: 2. Of those that a mesh axis runs over, the one named last changes fastest.
Arguments:
- cube: float32 [7077888], P(('groups', 'samp', 'line')), parts along dimension 0, may hold values from -4000 to 4000
Outputs:
- details1: float32 [5308416], P(('groups', 'samp', 'line')), parts along dimension 0
- details2: float32 [1327104], P(('groups', 'samp', 'line')), parts along dimension 0
- details3: float32 [331776], P(('groups', 'samp', 'line')), parts along dimension 0
- approx: float32 [110592], P(('groups', 'samp', 'line')), parts along dimension 0
The draws below stay inside these ranges and needn't reach their ends.
There are 2 independent parts, one for each index of `groups`. The reference program is written for one: setup_inputs(seed, part) draws one part's arguments, and reference() takes and returns one part's arrays. A program takes and returns all parts, laid end to end along the dimension named above; each array names one. Nothing has to cross between parts.
All inputs are finite; a program needn't handle non-finite values.
Results may differ from the reference program's by a relative error of at most 0.000088.
Values sent between devices are 32-bit elements; how exact they have to be, the bound alone decides.
A program may use at most 64 MiB of HBM per device.

```python
import math
import jax
import jax.numpy as jnp
from jax import lax

BANDS = 432
LD = 32
SD = 16
LINES = 64
SAMPLES = 128
NPIX = 8192
N_SAMP = 8
N_LINE = 2


def draw_cube(key, part):
    subkeys = jax.random.split(key, 4)
    log_ten = math.log(10.0)
    band_scale = jnp.exp(jax.random.uniform(subkeys[0], (BANDS, 1, 1), jnp.float32, 0.0, log_ten))
    offset = jax.random.uniform(subkeys[1], (BANDS, 1, 1), jnp.float32, -1.0, 1.0)
    sample_ramp = 1.0 + 2.0 * jnp.arange(SAMPLES, dtype=jnp.float32) / (SAMPLES - 1)
    pixel_scale = jnp.exp(jax.random.uniform(subkeys[2], (1, LINES, SAMPLES), jnp.float32, 0.0, log_ten)) * sample_ramp
    fresh_noise = jnp.clip(jax.random.normal(subkeys[3], (BANDS, LINES, SAMPLES), jnp.float32), -4.0, 4.0)
    common = jnp.zeros((1, LINES, SAMPLES), jnp.float32)
    blended = fresh_noise + 0.6 * jnp.roll(fresh_noise, 1, 0) + 0.4 * jnp.roll(fresh_noise, 2, 0)
    image = band_scale * (offset + common + pixel_scale * blended)
    shaped = image.reshape(BANDS, LINES // LD, LD, SAMPLES // SD, SD)
    return jnp.transpose(shaped, (3, 1, 0, 2, 4)).reshape(-1)


def setup_inputs(seed: int = 0, part: int = 0) -> dict:
    splits = jax.random.split(jax.random.key(seed), 2)
    part_splits = jax.random.split(jax.random.fold_in(splits[1], part), 2)
    return {
        "cube": draw_cube(jax.random.fold_in(jax.random.fold_in(splits[1], part), 71), part),
    }


alpha_lift = -1.586134342059924
beta_lift = -0.052980118572961
gamma_lift = 0.882911075530934
delta_lift = 0.443506852043971
scale_lift = 1.230174104914001

def split_pairs(values, axis):
    length = values.shape[axis]
    return (lax.slice_in_dim(values, 0, length, 2, axis), lax.slice_in_dim(values, 1, length, 2, axis))

def lift(values, axis):
    evens, odds = split_pairs(values, axis)
    half = evens.shape[axis]
    for weight_odd, weight_even in ((alpha_lift, beta_lift), (gamma_lift, delta_lift)):
        following = jnp.concatenate([lax.slice_in_dim(evens, 1, half, 1, axis), lax.slice_in_dim(evens, half - 1, half, 1, axis)], axis)
        odds = odds + weight_odd * (evens + following)
        preceding = jnp.concatenate([lax.slice_in_dim(odds, 0, 1, 1, axis), lax.slice_in_dim(odds, 0, half - 1, 1, axis)], axis)
        evens = evens + weight_even * (preceding + odds)
    return (evens / scale_lift, odds * scale_lift)

def subbands(values):
    low_s, high_s = lift(values, 2)
    low_l, high_l = lift(jnp.concatenate([low_s, high_s], 2), 1)
    middle = low_s.shape[2]
    details = jnp.stack([high_l[:, :, :middle], low_l[:, :, middle:], high_l[:, :, middle:]])
    return (low_l[:, :, :middle], details)

def to_tiles(values, level):
    tile_lines = LD // level
    tile_samples = SD // level
    lead = values.shape[:-2]
    count = len(lead)
    shaped = values.reshape(lead + (N_LINE, tile_lines, N_SAMP, tile_samples))
    order = (count + 2, count) + tuple(range(count)) + (count + 1, count + 3)
    return jnp.transpose(shaped, order).reshape(-1)

def reference(cube):
    tiled = cube.reshape(N_SAMP, N_LINE, BANDS, LD, SD)
    image = jnp.transpose(tiled, (2, 1, 3, 0, 4)).reshape(BANDS, LD * N_LINE, SD * N_SAMP)
    band_count = BANDS
    flattened = image.reshape(band_count, -1)
    band_mean = jnp.sum(flattened, axis=1) / NPIX
    centered = flattened - band_mean[:, None]
    covariance = jnp.dot(centered.astype(jnp.float32), centered.T.astype(jnp.float32), precision=lax.Precision.HIGHEST, preferred_element_type=jnp.float32) / NPIX
    identity = jnp.eye(band_count, dtype=covariance.dtype)
    regular = covariance + 0.01 * (jnp.trace(covariance) / band_count) * identity
    factor = jnp.linalg.cholesky(regular)
    whitener = lax.linalg.triangular_solve(factor, identity, left_side=True, lower=True)
    components = jnp.dot(whitener.astype(jnp.float32), centered.astype(jnp.float32), precision=lax.Precision.HIGHEST, preferred_element_type=jnp.float32).reshape(image.shape)
    approx1, level1 = subbands(components)
    approx2, level2 = subbands(approx1)
    approx3, level3 = subbands(approx2)
    return (to_tiles(level1, 2), to_tiles(level2, 4), to_tiles(level3, 8), to_tiles(approx3, 8))
```

```python
import functools
import jax
import jax.numpy as jnp
from jax import lax
from jax.experimental import pallas as pl
from jax.experimental.pallas import tpu as pltpu
from jax.sharding import PartitionSpec as P

BANDS = 432
LD = 32
SD = 16

MESH = pl.DeviceIdType.MESH
HIGH = lax.Precision.HIGHEST
LANES = 128
SUPER = 64


def blocks_of(bands):
    rows = [bands - start for start in range(0, bands, LANES)]
    offsets = [sum(rows[:i]) for i in range(len(rows))]
    return rows, offsets


alpha_lift = -1.586134342059924
beta_lift = -0.052980118572961
gamma_lift = 0.882911075530934
delta_lift = 0.443506852043971
scale_lift = 1.230174104914001
RIM = 4


def lift_list(values):
    evens, odds = values[0::2], values[1::2]
    odds = [o + alpha_lift * (e + f) for o, e, f in zip(odds[:-1], evens[:-1], evens[1:])]
    evens = [e + beta_lift * (o + q) for e, o, q in zip(evens[1:-1], odds[:-1], odds[1:])]
    odds = [o + gamma_lift * (e + f) for o, e, f in zip(odds[1:-1], evens[:-1], evens[1:])]
    evens = [e + delta_lift * (o + q) for e, o, q in zip(evens[1:-1], odds[:-1], odds[1:])]
    return [e * (1.0 / scale_lift) for e in evens], [o * scale_lift for o in odds[1:]]


def lift_lines(src, halo, dst, lines, width, ln):
    half = lines // 2
    for t in range(src.shape[0]):
        own = [src[t, i * width:(i + 1) * width] for i in range(lines)]
        got = [halo[t, i * width:(i + 1) * width] for i in range(RIM)]
        before = [jnp.where(ln == 0, own[RIM - i], got[i]) for i in range(RIM)]
        after = [jnp.where(ln == 0, got[i], own[lines - 2 - i]) for i in range(RIM)]
        low, high = lift_list(before + own + after)
        for i in range(half):
            dst[t, i * width:(i + 1) * width] = low[i]
            dst[t, (half + i) * width:(half + i + 1) * width] = high[i]


def rims(z, lines, width, left, right):
    for t in range(z.shape[0]):
        low = [z[t, pl.ds(s, lines, stride=width), :] for s in range(3)]
        top = [z[t, pl.ds(s, lines, stride=width), :] for s in range(width - 4, width)]
        left[t, :lines] = low[0]
        left[t, lines:] = low[0] + beta_lift * (low[1] + alpha_lift * (low[0] + low[2]))
        right[t, :lines] = top[3] + alpha_lift * top[2]
        right[t, lines:] = top[2] + beta_lift * (top[1] + alpha_lift * (top[0] + top[2]))


def lift_samples(z, from_left, from_right, lines, width, first, last, dests):
    half, n = lines // 2, width // 2
    for t in range(z.shape[0]):
        evens = [z[t, pl.ds(2 * i, lines, stride=width), :] for i in range(n)]
        odds = [z[t, pl.ds(2 * i + 1, lines, stride=width), :] for i in range(n)]
        beyond = jnp.where(last, evens[-1], from_right[t, :lines])
        odds1 = [o + alpha_lift * (e + f) for o, e, f in zip(odds, evens, evens[1:] + [beyond])]
        before = jnp.where(first, odds1[0], from_left[t, :lines] + alpha_lift * evens[0])
        evens1 = [e + beta_lift * (p + o) for e, p, o in zip(evens, [before] + odds1[:-1], odds1)]
        beyond = jnp.where(last, evens1[-1], from_right[t, lines:] + beta_lift * odds1[-1])
        odds2 = [o + gamma_lift * (e + f) for o, e, f in zip(odds1, evens1, evens1[1:] + [beyond])]
        outside = from_left[t, lines:] + beta_lift * before
        before = jnp.where(first, odds2[0], before + gamma_lift * (outside + evens1[0]))
        evens2 = [e + delta_lift * (p + o) for e, p, o in zip(evens1, [before] + odds2[:-1], odds2)]
        for i in range(n):
            low, high = evens2[i] * (1.0 / scale_lift), odds2[i] * scale_lift
            for (ref, base), value in zip(dests, (low[:half], low[half:], high[:half], high[half:])):
                ref[t, pl.ds(base + i, half, stride=n), :] = value


def split3(value):
    first = value.astype(jnp.bfloat16).astype(jnp.float32)
    rest = value - first
    second = rest.astype(jnp.bfloat16).astype(jnp.float32)
    return first, second, rest - second


def gram_kernel(samp, line, bands, lines, width, x_ref, o1_ref, o2_ref, o3_ref, o4_ref, t_ref, m, rest, corr, v1, v2, v3, z1, z2, z3, n1, n2, n3, el1, er1, el2, er2, el3, er3, fl1, fr1, fl2, fr2, fl3, fr3,
                l_send, l_recv, r_send, r_recv, xs, sums, sums_in, g, half_in,
                chunk_in, tot, s_send, s_recv, h_send, h_recv, c_send, c_recv, a_send, a_recv,
                b_send, b_recv):
    me, ln = lax.axis_index("samp"), lax.axis_index("line")
    devices = samp * line
    pixels = lines * width
    first, last = me == 0, me == samp - 1
    flat = me * line + ln
    packs = pixels // LANES
    padded = xs.shape[0]

    def peer(d):
        other = lax.rem(flat + d, devices)
        return {"samp": other // line, "line": lax.rem(other, line)}

    def line_copy(level, src, dst, tall, wide):
        rows = RIM * wide
        start = pl.multiple_of((1 - ln) * ((tall - RIM) * wide), 8)
        copy = pltpu.make_async_remote_copy(src.at[:, pl.ds(start, rows)], dst, l_send.at[level], l_recv.at[level],
                                            device_id={"line": 1 - ln}, device_id_type=MESH)
        copy.start()
        return copy

    def rim_copies(level, left, right, from_left, from_right):
        below = pltpu.make_async_remote_copy(left, from_right, r_send.at[level, 0], r_recv.at[level, 0],
                                             device_id={"samp": jnp.maximum(me - 1, 0)}, device_id_type=MESH)
        above = pltpu.make_async_remote_copy(right, from_left, r_send.at[level, 1], r_recv.at[level, 1],
                                             device_id={"samp": jnp.minimum(me + 1, samp - 1)}, device_id_type=MESH)

        @pl.when(me > 0)
        def _():
            below.start()

        @pl.when(me < samp - 1)
        def _():
            above.start()

        return below, above

    def rim_wait(pair):
        below, above = pair

        @pl.when(me > 0)
        def _():
            below.wait_send()
            above.wait_recv()

        @pl.when(me < samp - 1)
        def _():
            above.wait_send()
            below.wait_recv()

    for ref in (fl1, fr1, fl2, fr2, fl3, fr3):
        ref[...] = jnp.zeros_like(ref)
    barrier = pltpu.get_barrier_semaphore()
    for d in range(1, devices):
        pl.semaphore_signal(barrier, inc=1, device_id=peer(d), device_id_type=MESH)
    if padded > bands:
        xs[bands:, :] = jnp.zeros((padded - bands, pixels), jnp.float32)
    for q in range(packs):
        xs[0:bands, q * LANES:(q + 1) * LANES] = x_ref[pl.ds(q, bands, stride=packs), :]
    sums[...] = lax.dot_general(jnp.ones((8, pixels), jnp.float32), xs[...], (((1,), (1,)), ((), ())),
                                precision=HIGH, preferred_element_type=jnp.float32)[0:1]
    pl.semaphore_wait(barrier, devices - 1)
    copies = []
    for d in range(1, devices):
        copy = pltpu.make_async_remote_copy(sums, sums_in.at[d - 1], s_send.at[d - 1], s_recv.at[d - 1],
                                            device_id=peer(d), device_id_type=MESH)
        copy.start()
        copies.append(copy)
    sum_copies = copies
    local_mean = sums[...] / float(pixels)
    xs[...] = xs[...] - jnp.transpose(jnp.broadcast_to(local_mean, (8, padded)))[:, 0:1]
    rows, offsets = blocks_of(bands)
    for q, (count, offset) in enumerate(zip(rows, offsets)):
        g[offset:offset + count, :] = lax.dot_general(
            xs[q * LANES:q * LANES + count, :], xs[q * LANES:(q + 1) * LANES, :],
            (((1,), (1,)), ((), ())), precision=HIGH, preferred_element_type=jnp.float32)
    used = offsets[-1] + rows[-1]
    if g.shape[0] > used:
        g[used:, :] = jnp.zeros((g.shape[0] - used, LANES), jnp.float32)
    half = g.shape[0] // line
    chunk = half // samp
    copies = []
    for d in range(1, line):
        other = lax.rem(ln + d, line)
        copy = pltpu.make_async_remote_copy(
            g.at[pl.ds(pl.multiple_of(other * half, 8), half)], half_in.at[d - 1], h_send.at[d - 1],
            h_recv.at[d - 1], device_id={"line": other}, device_id_type=MESH)
        copy.start()
        copies.append(copy)
    for copy in copies:
        copy.wait()
    mine = pl.ds(pl.multiple_of(ln * half, 8), half)
    value = g[mine, :]
    for d in range(1, line):
        value = value + half_in[d - 1]
    g[mine, :] = value
    copies = []
    for d in range(1, samp):
        other = lax.rem(me + d, samp)
        copy = pltpu.make_async_remote_copy(
            g.at[pl.ds(pl.multiple_of(ln * half + other * chunk, 8), chunk)], chunk_in.at[d - 1],
            c_send.at[d - 1], c_recv.at[d - 1], device_id={"samp": other}, device_id_type=MESH)
        copy.start()
        copies.append(copy)
    for copy in sum_copies:
        copy.wait()
    total = sums[...]
    for d in range(1, devices):
        total = total + sums_in[d - 1]
    mean = total / float(pixels * devices)
    spread = jnp.concatenate([local_mean - mean] + [sums_in[d - 1] / float(pixels) - mean
                                                    for d in range(1, devices)], axis=0)
    shift = local_mean - mean
    for t in range(v1.shape[0]):
        v1[t] = jnp.transpose(xs[t * LANES:(t + 1) * LANES, :]) + shift[:, t * LANES:(t + 1) * LANES]
    lines1 = line_copy(0, v1, n1, lines, width)
    for q, (count, offset) in enumerate(zip(rows, offsets)):
        corr[offset:offset + count, :] = float(pixels) * lax.dot_general(
            spread, spread[:, q * LANES:(q + 1) * LANES], (((0,), (0,)), ((), ())), precision=HIGH,
            preferred_element_type=jnp.float32)[q * LANES:q * LANES + count]
    if g.shape[0] > used:
        corr[used:, :] = jnp.zeros((g.shape[0] - used, LANES), jnp.float32)
    lines1.wait()
    lift_lines(v1, n1, z1, lines, width, ln)
    rims(z1, lines, width, el1, er1)
    for copy in copies:
        copy.wait()
    own = pl.ds(pl.multiple_of(ln * half + me * chunk, 8), chunk)
    value = g[own, :] + corr[own, :]
    for d in range(1, samp):
        value = value + chunk_in[d - 1]
    tot[own, :] = value
    copies = []
    for d in range(1, samp):
        other = lax.rem(me + d, samp)
        copy = pltpu.make_async_remote_copy(tot.at[own], tot.at[own], a_send.at[d - 1], a_recv.at[d - 1],
                                            device_id={"samp": other}, device_id_type=MESH)
        copy.start()
        copies.append(copy)
    pair = rim_copies(0, el1, er1, fl1, fr1)
    for copy in copies:
        copy.wait()
    copies = []
    for d in range(1, line):
        other = lax.rem(ln + d, line)
        copy = pltpu.make_async_remote_copy(tot.at[mine], tot.at[mine], b_send.at[d - 1], b_recv.at[d - 1],
                                            device_id={"line": other}, device_id_type=MESH)
        copy.start()
        copies.append(copy)
    for copy in copies:
        copy.wait()
    wide = m.shape[1]
    rows, offsets = blocks_of(bands)
    diag = lax.broadcasted_iota(jnp.int32, (LANES, LANES), 0) == lax.broadcasted_iota(
        jnp.int32, (LANES, LANES), 1)
    scale = 1.0 / float(pixels * devices)
    trace = jnp.zeros((1, 1), jnp.float32)
    for q, offset in enumerate(offsets):
        size = min(LANES, rows[q])
        block = tot[offset:offset + size, :]
        kept = jnp.where(diag[:size], block, 0.0)
        trace = trace + jnp.sum(jnp.sum(kept, axis=0, keepdims=True), axis=1, keepdims=True)
    ridge = trace * scale * (0.01 / bands)
    for q, offset in enumerate(offsets):
        for b in range(q, len(rows)):
            size = min(LANES, rows[b])
            start = offset + (b - q) * LANES
            block = tot[start:start + size, :] * scale
            if b == q:
                low = jnp.where(diag[:size], block + ridge, block)
                m[q * LANES:q * LANES + size, q * LANES:(q + 1) * LANES] = low
            else:
                if size < LANES:
                    block = jnp.concatenate([block, jnp.zeros((LANES - size, LANES), jnp.float32)], axis=0)
                m[q * LANES:(q + 1) * LANES, b * LANES:(b + 1) * LANES] = jnp.transpose(block)
                m[b * LANES:b * LANES + size, q * LANES:(q + 1) * LANES] = block[:size]
    sub = lax.broadcasted_iota(jnp.int32, (8, LANES), 0)
    lane = lax.broadcasted_iota(jnp.int32, (8, LANES), 1)
    tiles = wide // LANES

    def superblock(start):
        size = min(SUPER, bands - start)
        count = size // 8
        panels = [[m[start + 8 * i:start + 8 * i + 8, t * LANES:(t + 1) * LANES] for t in range(tiles)]
                  for i in range(count)]
        done = []
        for k in range(count):
            top = start + 8 * k
            at, lane0 = top // LANES, top % LANES
            own = panels[k]
            cols = [jnp.broadcast_to(own[at][:, lane0 + e:lane0 + e + 1], (8, LANES)) for e in range(8)]
            later = range(k + 1, count)
            below = {p: [jnp.broadcast_to(panels[p][at][:, lane0 + e:lane0 + e + 1], (8, LANES)) for e in range(8)]
                     for p in later}
            inside = (lane >= lane0) & (lane < lane0 + 8)
            own[at] = jnp.where(inside, jnp.where(lane - lane0 == sub, 1.0, 0.0), own[at])
            for p in later:
                panels[p][at] = jnp.where(inside, 0.0, panels[p][at])
            pivots = None
            for b in range(8):
                pivot = jnp.broadcast_to(cols[b][b:b + 1, :], (8, LANES))
                inverse = 1.0 / pivot
                pivots = pivot if pivots is None else jnp.where(sub == b, pivot, pivots)
                factor = jnp.where(sub > b, cols[b] * inverse, 0.0)
                rows_b = [jnp.broadcast_to(own[t][b:b + 1, :], (8, LANES)) for t in range(tiles)]
                heads = {e: jnp.broadcast_to(cols[e][b:b + 1, :], (8, LANES)) for e in range(b + 1, 8)}
                for e in range(b + 1, 8):
                    cols[e] = cols[e] - factor * heads[e]
                for p in later:
                    scaled = below[p][b] * inverse
                    for e in range(b + 1, 8):
                        below[p][e] = below[p][e] - scaled * heads[e]
                    for t in range(tiles):
                        panels[p][t] = panels[p][t] - scaled * rows_b[t]
                if b < 7:
                    for t in range(tiles):
                        own[t] = own[t] - factor * rows_b[t]
            root = lax.rsqrt(pivots)
            done.append([own[t] * root for t in range(tiles)])
            for t in range(tiles):
                m[top:top + 8, t * LANES:(t + 1) * LANES] = done[k][t]
        below_at = start + size
        if below_at >= bands:
            return
        full = [jnp.concatenate([done[k][t] for k in range(count)], axis=0) for t in range(tiles)]
        kept = list(full)
        row_ids = lax.broadcasted_iota(jnp.int32, (size, LANES), 0) + start % LANES
        lane_ids = lax.broadcasted_iota(jnp.int32, (size, LANES), 1)
        upper = (lane_ids > row_ids) & (lane_ids < start % LANES + size)
        kept[start // LANES] = jnp.where(upper, 0.0, kept[start // LANES])
        splits = [split3(part) for part in kept]
        right = jnp.concatenate(
            [jnp.concatenate([splits[t][0], splits[t][0], splits[t][0], splits[t][1], splits[t][2], splits[t][1]], axis=0)
             for t in range(tiles)], axis=1).astype(jnp.bfloat16)
        half_lanes = lax.broadcasted_iota(jnp.int32, (LANES, LANES), 1) < size
        for t in range(below_at // LANES, tiles):
            flipped = jnp.transpose(jnp.concatenate([full[t], full[t]], axis=0))
            one, two, three = split3(flipped)
            first_pair = jnp.where(half_lanes, one, two)
            second_pair = jnp.where(half_lanes, three, one)
            left = jnp.concatenate([first_pair, second_pair, first_pair], axis=1).astype(jnp.bfloat16)
            lo = max(below_at, t * LANES)
            bounds = [lo]
            while bounds[-1] < min(bands, (t + 1) * LANES):
                bounds.append(min(bounds[-1] + SUPER, bands, (t + 1) * LANES))
            for low_row, high_row in zip(bounds[:-1], bounds[1:]):
                update = lax.dot_general(
                    left[low_row - t * LANES:high_row - t * LANES], right, (((1,), (0,)), ((), ())),
                    preferred_element_type=jnp.float32)
                for u in range(tiles):
                    old = m[low_row:high_row, u * LANES:(u + 1) * LANES]
                    if start // LANES == u:
                        lanes = lax.broadcasted_iota(jnp.int32, (high_row - low_row, LANES), 1)
                        old = jnp.where((lanes >= start % LANES) & (lanes < start % LANES + size), 0.0, old)
                    m[low_row:high_row, u * LANES:(u + 1) * LANES] = old - update[:, u * LANES:(u + 1) * LANES]

    def eliminate(c):
        for start in range(c * LANES, min(bands, (c + 1) * LANES), SUPER):
            superblock(start)

    eliminate(0)
    rim_wait(pair)
    h, w = lines // 2, width // 2
    one = h * w
    lift_samples(z1, fl1, fr1, lines, width, first, last, ((v2, 0), (t_ref, 0), (t_ref, one), (t_ref, 2 * one)))
    lines2 = line_copy(1, v2, n2, h, w)
    eliminate(1)
    lines2.wait()
    lift_lines(v2, n2, z2, h, w, ln)
    rims(z2, h, w, el2, er2)
    pair2 = rim_copies(1, el2, er2, fl2, fr2)
    eliminate(2)
    rim_wait(pair2)
    two, base2 = one // 4, 3 * one
    lift_samples(z2, fl2, fr2, h, w, first, last,
                 ((v3, 0), (t_ref, base2), (t_ref, base2 + two), (t_ref, base2 + 2 * two)))
    h, w = h // 2, w // 2
    lines3 = line_copy(2, v3, n3, h, w)
    lines3.wait()
    lift_lines(v3, n3, z3, h, w, ln)
    rims(z3, h, w, el3, er3)
    pair3 = rim_copies(2, el3, er3, fl3, fr3)
    for c in range(3, len(rows)):
        eliminate(c)
    rim_wait(pair3)
    three, base3 = two // 4, base2 + 3 * two
    lift_samples(z3, fl3, fr3, h, w, first, last,
                 ((t_ref, base3 + 3 * three), (t_ref, base3), (t_ref, base3 + three), (t_ref, base3 + 2 * three)))
    keep = lax.broadcasted_iota(jnp.int32, (bands, wide), 1) <= lax.broadcasted_iota(
        jnp.int32, (bands, wide), 0)
    m[...] = jnp.where(keep, m[...], 0.0)
    for q in range(t_ref.shape[1] // LANES):
        part = jnp.concatenate([t_ref[t, q * LANES:(q + 1) * LANES, :] for t in range(wide // LANES)], axis=1)
        out = lax.dot_general(m[...], part, (((1,), (1,)), ((), ())),
                              precision=HIGH, preferred_element_type=jnp.float32)
        if q < o1_ref.shape[0]:
            o1_ref[q] = out
        else:
            rest[...] = out


    def pack(dest, at, lane0, wide_out):
        group = LANES // wide_out
        count = bands // group
        pieces = [rest[pl.ds(b, count, stride=group), :][:, lane0:lane0 + wide_out] for b in range(group)]
        dest[at:at + count, :] = jnp.concatenate(pieces, axis=1)

    for i in range(3):
        pack(o2_ref, i * (o2_ref.shape[0] // 3), i * two, two)
        pack(o3_ref, i * (o3_ref.shape[0] // 3), 3 * two + i * three, three)
    pack(o4_ref, 0, 3 * two + 3 * three, three)


def gram_call(cube, bands, lines, width):
    pixels = lines * width
    samp, line = lax.axis_size("samp"), lax.axis_size("line")
    devices = samp * line
    rows, offsets = blocks_of(bands)
    used = offsets[-1] + rows[-1]
    unit = 8 * devices
    total = -(-used // unit) * unit
    padded = -(-bands // LANES) * LANES
    f32 = jnp.float32
    sem = pltpu.SemaphoreType.DMA
    return pl.pallas_call(
        functools.partial(gram_kernel, samp, line, bands, lines, width),
        out_shape=(jax.ShapeDtypeStruct((3, bands, LANES), f32),
                   jax.ShapeDtypeStruct((3 * bands * (pixels // 16) // LANES, LANES), f32),
                   jax.ShapeDtypeStruct((3 * bands * (pixels // 64) // LANES, LANES), f32),
                   jax.ShapeDtypeStruct((bands * (pixels // 64) // LANES, LANES), f32)),
        in_specs=[pl.BlockSpec(memory_space=pltpu.VMEM)],
        out_specs=(pl.BlockSpec(memory_space=pltpu.VMEM),) * 4,
        scratch_shapes=[
            pltpu.VMEM((padded // LANES, pixels, LANES), f32), pltpu.VMEM((bands, padded), f32),
            pltpu.VMEM((bands, LANES), f32), pltpu.VMEM((total, LANES), f32),
            *[pltpu.VMEM((padded // LANES, pixels // 4 ** i, LANES), f32) for i in (0, 1, 2)],
            *[pltpu.VMEM((padded // LANES, pixels // 4 ** i, LANES), f32) for i in (0, 1, 2)],
            *[pltpu.VMEM((padded // LANES, RIM * width // 2 ** i, LANES), f32) for i in (0, 1, 2)],
            *[pltpu.VMEM((padded // LANES, 2 * lines // 2 ** i, LANES), f32) for i in (0, 0, 1, 1, 2, 2)],
            *[pltpu.VMEM((padded // LANES, 2 * lines // 2 ** i, LANES), f32) for i in (0, 0, 1, 1, 2, 2)],
            sem((3,)), sem((3,)), sem((3, 2)), sem((3, 2)),
            pltpu.VMEM((padded, pixels), f32), pltpu.VMEM((1, padded), f32),
            pltpu.VMEM((devices - 1, 1, padded), f32), pltpu.VMEM((total, LANES), f32),
            pltpu.VMEM((line - 1, total // line, LANES), f32),
            pltpu.VMEM((samp - 1, total // devices, LANES), f32), pltpu.VMEM((total, LANES), f32),
            sem((devices - 1,)), sem((devices - 1,)), sem((line - 1,)), sem((line - 1,)),
            sem((samp - 1,)), sem((samp - 1,)), sem((samp - 1,)), sem((samp - 1,)),
            sem((line - 1,)), sem((line - 1,)),
        ],
        compiler_params=pltpu.CompilerParams(collective_id=0, has_side_effects=True),
    )(cube.reshape(-1, LANES))


def local(cube):
    return tuple(out.reshape(-1) for out in gram_call(cube, BANDS, LD, SD))


def solution(mesh):
    in_specs = (P(("groups", "samp", "line")),)
    out_specs = (
        P(("groups", "samp", "line")),
        P(("groups", "samp", "line")),
        P(("groups", "samp", "line")),
        P(("groups", "samp", "line")),
    )
    return jax.shard_map(local, mesh=mesh, in_specs=in_specs, out_specs=out_specs, check_vma=False)
```

```python
import functools
import jax
import jax.numpy as jnp
from jax import lax
from jax.experimental import pallas as pl
from jax.experimental.pallas import tpu as pltpu
from jax.sharding import PartitionSpec as P

BANDS = 432
LD = 32
SD = 16

MESH = pl.DeviceIdType.MESH
HIGH = lax.Precision.HIGHEST
LANES = 128
SUPER = 64


def blocks_of(bands):
    rows = [bands - start for start in range(0, bands, LANES)]
    offsets = [sum(rows[:i]) for i in range(len(rows))]
    return rows, offsets


alpha_lift = -1.586134342059924
beta_lift = -0.052980118572961
gamma_lift = 0.882911075530934
delta_lift = 0.443506852043971
scale_lift = 1.230174104914001
RIM = 4


def lift_list(values):
    evens, odds = values[0::2], values[1::2]
    odds = [o + alpha_lift * (e + f) for o, e, f in zip(odds[:-1], evens[:-1], evens[1:])]
    evens = [e + beta_lift * (o + q) for e, o, q in zip(evens[1:-1], odds[:-1], odds[1:])]
    odds = [o + gamma_lift * (e + f) for o, e, f in zip(odds[1:-1], evens[:-1], evens[1:])]
    evens = [e + delta_lift * (o + q) for e, o, q in zip(evens[1:-1], odds[:-1], odds[1:])]
    return [e * (1.0 / scale_lift) for e in evens], [o * scale_lift for o in odds[1:]]


def lift_lines(src, halo, dst, lines, width, ln):
    half = lines // 2
    for t in range(src.shape[0]):
        own = [src[t, i * width:(i + 1) * width] for i in range(lines)]
        got = [halo[t, i * width:(i + 1) * width] for i in range(RIM)]
        before = [jnp.where(ln == 0, own[RIM - i], got[i]) for i in range(RIM)]
        after = [jnp.where(ln == 0, got[i], own[lines - 2 - i]) for i in range(RIM)]
        low, high = lift_list(before + own + after)
        for i in range(half):
            dst[t, i * width:(i + 1) * width] = low[i]
            dst[t, (half + i) * width:(half + i + 1) * width] = high[i]


def rims(z, lines, width, left, right):
    for t in range(z.shape[0]):
        low = [z[t, pl.ds(s, lines, stride=width), :] for s in range(3)]
        top = [z[t, pl.ds(s, lines, stride=width), :] for s in range(width - 4, width)]
        left[t, :lines] = low[0]
        left[t, lines:] = low[0] + beta_lift * (low[1] + alpha_lift * (low[0] + low[2]))
        right[t, :lines] = top[3] + alpha_lift * top[2]
        right[t, lines:] = top[2] + beta_lift * (top[1] + alpha_lift * (top[0] + top[2]))


def lift_samples(z, from_left, from_right, lines, width, first, last, dests):
    half, n = lines // 2, width // 2
    for t in range(z.shape[0]):
        evens = [z[t, pl.ds(2 * i, lines, stride=width), :] for i in range(n)]
        odds = [z[t, pl.ds(2 * i + 1, lines, stride=width), :] for i in range(n)]
        beyond = jnp.where(last, evens[-1], from_right[t, :lines])
        odds1 = [o + alpha_lift * (e + f) for o, e, f in zip(odds, evens, evens[1:] + [beyond])]
        before = jnp.where(first, odds1[0], from_left[t, :lines] + alpha_lift * evens[0])
        evens1 = [e + beta_lift * (p + o) for e, p, o in zip(evens, [before] + odds1[:-1], odds1)]
        beyond = jnp.where(last, evens1[-1], from_right[t, lines:] + beta_lift * odds1[-1])
        odds2 = [o + gamma_lift * (e + f) for o, e, f in zip(odds1, evens1, evens1[1:] + [beyond])]
        outside = from_left[t, lines:] + beta_lift * before
        before = jnp.where(first, odds2[0], before + gamma_lift * (outside + evens1[0]))
        evens2 = [e + delta_lift * (p + o) for e, p, o in zip(evens1, [before] + odds2[:-1], odds2)]
        for i in range(n):
            low, high = evens2[i] * (1.0 / scale_lift), odds2[i] * scale_lift
            for (ref, base), value in zip(dests, (low[:half], low[half:], high[:half], high[half:])):
                ref[t, pl.ds(base + i, half, stride=n), :] = value


def split3(value):
    first = value.astype(jnp.bfloat16).astype(jnp.float32)
    rest = value - first
    second = rest.astype(jnp.bfloat16).astype(jnp.float32)
    return first, second, rest - second


def gram_kernel(samp, line, bands, lines, width, x_ref, o1_ref, o2_ref, o3_ref, o4_ref, t_ref, th, tl, m, rest, corr, v1, v2, v3, z1, z2, z3, n1, n2, n3, el1, er1, el2, er2, el3, er3, fl1, fr1, fl2, fr2, fl3, fr3,
                l_send, l_recv, r_send, r_recv, xs, sums, sums_in, g, half_in,
                chunk_in, tot, s_send, s_recv, h_send, h_recv, c_send, c_recv, a_send, a_recv,
                b_send, b_recv):
    me, ln = lax.axis_index("samp"), lax.axis_index("line")
    devices = samp * line
    pixels = lines * width
    first, last = me == 0, me == samp - 1
    flat = me * line + ln
    packs = pixels // LANES
    padded = xs.shape[0]

    def peer(d):
        other = lax.rem(flat + d, devices)
        return {"samp": other // line, "line": lax.rem(other, line)}

    def line_copy(level, src, dst, tall, wide):
        rows = RIM * wide
        start = pl.multiple_of((1 - ln) * ((tall - RIM) * wide), 8)
        copy = pltpu.make_async_remote_copy(src.at[:, pl.ds(start, rows)], dst, l_send.at[level], l_recv.at[level],
                                            device_id={"line": 1 - ln}, device_id_type=MESH)
        copy.start()
        return copy

    def rim_copies(level, left, right, from_left, from_right):
        below = pltpu.make_async_remote_copy(left, from_right, r_send.at[level, 0], r_recv.at[level, 0],
                                             device_id={"samp": jnp.maximum(me - 1, 0)}, device_id_type=MESH)
        above = pltpu.make_async_remote_copy(right, from_left, r_send.at[level, 1], r_recv.at[level, 1],
                                             device_id={"samp": jnp.minimum(me + 1, samp - 1)}, device_id_type=MESH)

        @pl.when(me > 0)
        def _():
            below.start()

        @pl.when(me < samp - 1)
        def _():
            above.start()

        return below, above

    def rim_wait(pair):
        below, above = pair

        @pl.when(me > 0)
        def _():
            below.wait_send()
            above.wait_recv()

        @pl.when(me < samp - 1)
        def _():
            above.wait_send()
            below.wait_recv()

    for ref in (fl1, fr1, fl2, fr2, fl3, fr3):
        ref[...] = jnp.zeros_like(ref)
    barrier = pltpu.get_barrier_semaphore()
    for d in range(1, devices):
        pl.semaphore_signal(barrier, inc=1, device_id=peer(d), device_id_type=MESH)
    if padded > bands:
        xs[bands:, :] = jnp.zeros((padded - bands, pixels), jnp.float32)
    parts = [x_ref[pl.ds(q, bands, stride=packs), :] for q in range(packs)]
    folded = parts[0]
    for part in parts[1:]:
        folded = folded + part
    if padded > bands:
        folded = jnp.concatenate([folded, jnp.zeros((padded - bands, LANES), jnp.float32)], axis=0)
    folded = jnp.concatenate(split3(folded), axis=1).astype(jnp.bfloat16)
    sums[...] = lax.dot_general(jnp.ones((8, 3 * LANES), jnp.bfloat16), folded, (((1,), (1,)), ((), ())),
                                preferred_element_type=jnp.float32)[0:1]
    centre = lax.dot_general(folded[0:bands], jnp.ones((3 * LANES, LANES), jnp.bfloat16), (((1,), (0,)), ((), ())),
                             preferred_element_type=jnp.float32) / float(pixels)
    for q in range(packs):
        xs[0:bands, q * LANES:(q + 1) * LANES] = parts[q] - centre
    pl.semaphore_wait(barrier, devices - 1)
    copies = []
    for d in range(1, devices):
        copy = pltpu.make_async_remote_copy(sums, sums_in.at[d - 1], s_send.at[d - 1], s_recv.at[d - 1],
                                            device_id=peer(d), device_id_type=MESH)
        copy.start()
        copies.append(copy)
    sum_copies = copies
    local_mean = sums[...] / float(pixels)
    rows, offsets = blocks_of(bands)
    coarse = xs[...].astype(jnp.bfloat16)
    fine = (xs[...] - coarse.astype(jnp.float32)).astype(jnp.bfloat16)
    tall = jnp.concatenate([coarse, coarse, fine, fine], axis=1)
    flat_right = jnp.concatenate([coarse, fine, coarse, fine], axis=1)
    for q in range(0, len(rows), 2):
        span = min(2 * LANES, padded - q * LANES)
        both = lax.dot_general(tall[q * LANES:bands], flat_right[q * LANES:q * LANES + span],
                               (((1,), (1,)), ((), ())), preferred_element_type=jnp.float32)
        for b in range(span // LANES):
            g[offsets[q + b]:offsets[q + b] + rows[q + b], :] = both[b * LANES:, b * LANES:(b + 1) * LANES]
    used = offsets[-1] + rows[-1]
    if g.shape[0] > used:
        g[used:, :] = jnp.zeros((g.shape[0] - used, LANES), jnp.float32)
    half = g.shape[0] // line
    chunk = half // samp
    copies = []
    for d in range(1, line):
        other = lax.rem(ln + d, line)
        copy = pltpu.make_async_remote_copy(
            g.at[pl.ds(pl.multiple_of(other * half, 8), half)], half_in.at[d - 1], h_send.at[d - 1],
            h_recv.at[d - 1], device_id={"line": other}, device_id_type=MESH)
        copy.start()
        copies.append(copy)
    for copy in copies:
        copy.wait()
    mine = pl.ds(pl.multiple_of(ln * half, 8), half)
    value = g[mine, :]
    for d in range(1, line):
        value = value + half_in[d - 1]
    g[mine, :] = value
    copies = []
    for d in range(1, samp):
        other = lax.rem(me + d, samp)
        copy = pltpu.make_async_remote_copy(
            g.at[pl.ds(pl.multiple_of(ln * half + other * chunk, 8), chunk)], chunk_in.at[d - 1],
            c_send.at[d - 1], c_recv.at[d - 1], device_id={"samp": other}, device_id_type=MESH)
        copy.start()
        copies.append(copy)
    for copy in sum_copies:
        copy.wait()
    total = sums[...]
    for d in range(1, devices):
        total = total + sums_in[d - 1]
    mean = total / float(pixels * devices)
    spread = jnp.concatenate([local_mean - mean] + [sums_in[d - 1] / float(pixels) - mean
                                                    for d in range(1, devices)], axis=0)
    shift = local_mean - mean
    for t in range(v1.shape[0]):
        v1[t] = jnp.transpose(xs[t * LANES:(t + 1) * LANES, :]) + shift[:, t * LANES:(t + 1) * LANES]
    lines1 = line_copy(0, v1, n1, lines, width)
    for q, (count, offset) in enumerate(zip(rows, offsets)):
        corr[offset:offset + count, :] = float(pixels) * lax.dot_general(
            spread, spread[:, q * LANES:(q + 1) * LANES], (((0,), (0,)), ((), ())), precision=HIGH,
            preferred_element_type=jnp.float32)[q * LANES:q * LANES + count]
    if g.shape[0] > used:
        corr[used:, :] = jnp.zeros((g.shape[0] - used, LANES), jnp.float32)
    lines1.wait()
    lift_lines(v1, n1, z1, lines, width, ln)
    rims(z1, lines, width, el1, er1)
    for copy in copies:
        copy.wait()
    own = pl.ds(pl.multiple_of(ln * half + me * chunk, 8), chunk)
    value = g[own, :] + corr[own, :]
    for d in range(1, samp):
        value = value + chunk_in[d - 1]
    tot[own, :] = value
    copies = []
    for d in range(1, samp):
        other = lax.rem(me + d, samp)
        copy = pltpu.make_async_remote_copy(tot.at[own], tot.at[own], a_send.at[d - 1], a_recv.at[d - 1],
                                            device_id={"samp": other}, device_id_type=MESH)
        copy.start()
        copies.append(copy)
    pair = rim_copies(0, el1, er1, fl1, fr1)
    for copy in copies:
        copy.wait()
    copies = []
    for d in range(1, line):
        other = lax.rem(ln + d, line)
        copy = pltpu.make_async_remote_copy(tot.at[mine], tot.at[mine], b_send.at[d - 1], b_recv.at[d - 1],
                                            device_id={"line": other}, device_id_type=MESH)
        copy.start()
        copies.append(copy)
    for copy in copies:
        copy.wait()
    wide = m.shape[1]
    rows, offsets = blocks_of(bands)
    diag = lax.broadcasted_iota(jnp.int32, (LANES, LANES), 0) == lax.broadcasted_iota(
        jnp.int32, (LANES, LANES), 1)
    scale = 1.0 / float(pixels * devices)
    trace = jnp.zeros((1, 1), jnp.float32)
    for q, offset in enumerate(offsets):
        size = min(LANES, rows[q])
        block = tot[offset:offset + size, :]
        kept = jnp.where(diag[:size], block, 0.0)
        trace = trace + jnp.sum(jnp.sum(kept, axis=0, keepdims=True), axis=1, keepdims=True)
    ridge = trace * scale * (0.01 / bands)
    for q, offset in enumerate(offsets):
        for b in range(q, len(rows)):
            size = min(LANES, rows[b])
            start = offset + (b - q) * LANES
            block = tot[start:start + size, :] * scale
            if b == q:
                low = jnp.where(diag[:size], block + ridge, block)
                m[q * LANES:q * LANES + size, q * LANES:(q + 1) * LANES] = low
            else:
                if size < LANES:
                    block = jnp.concatenate([block, jnp.zeros((LANES - size, LANES), jnp.float32)], axis=0)
                m[q * LANES:(q + 1) * LANES, b * LANES:(b + 1) * LANES] = jnp.transpose(block)
                m[b * LANES:b * LANES + size, q * LANES:(q + 1) * LANES] = block[:size]
    sub = lax.broadcasted_iota(jnp.int32, (8, LANES), 0)
    lane = lax.broadcasted_iota(jnp.int32, (8, LANES), 1)
    tiles = wide // LANES

    def superblock(start):
        size = min(SUPER, bands - start)
        count = size // 8
        panels = [[m[start + 8 * i:start + 8 * i + 8, t * LANES:(t + 1) * LANES] for t in range(tiles)]
                  for i in range(count)]
        done = []

        def spread(tile, lane0):
            return [jnp.broadcast_to(tile[:, lane0 + e:lane0 + e + 1], (8, LANES)) for e in range(8)]

        ahead = spread(panels[0][start // LANES], start % LANES)
        for k in range(count):
            top = start + 8 * k
            at, lane0 = top // LANES, top % LANES
            own = panels[k]
            cols = ahead
            if k + 1 < count:
                ahead = spread(panels[k + 1][(top + 8) // LANES], (top + 8) % LANES)
            later = range(k + 1, count)
            below = {p: [jnp.broadcast_to(panels[p][at][:, lane0 + e:lane0 + e + 1], (8, LANES)) for e in range(8)]
                     for p in later}
            inside = (lane >= lane0) & (lane < lane0 + 8)
            own[at] = jnp.where(inside, jnp.where(lane - lane0 == sub, 1.0, 0.0), own[at])
            for p in later:
                panels[p][at] = jnp.where(inside, 0.0, panels[p][at])
            pivots = None
            for b in range(8):
                pivot = jnp.broadcast_to(cols[b][b:b + 1, :], (8, LANES))
                inverse = 1.0 / pivot
                pivots = pivot if pivots is None else jnp.where(sub == b, pivot, pivots)
                factor = jnp.where(sub > b, cols[b] * inverse, 0.0)
                rows_b = [jnp.broadcast_to(own[t][b:b + 1, :], (8, LANES)) for t in range(tiles)]
                heads = {e: jnp.broadcast_to(cols[e][b:b + 1, :], (8, LANES)) for e in range(b + 1, 8)}
                for e in range(b + 1, 8):
                    cols[e] = cols[e] - factor * heads[e]
                for p in later:
                    scaled = below[p][b] * inverse
                    if p == k + 1:
                        ahead = [ahead[e] - scaled * jnp.broadcast_to(below[p][b][e:e + 1, :], (8, LANES))
                                 for e in range(8)]
                    for e in range(b + 1, 8):
                        below[p][e] = below[p][e] - scaled * heads[e]
                    for t in range(tiles):
                        panels[p][t] = panels[p][t] - scaled * rows_b[t]
                if b < 7:
                    for t in range(tiles):
                        own[t] = own[t] - factor * rows_b[t]
            root = lax.rsqrt(pivots)
            done.append([own[t] * root for t in range(tiles)])
            for t in range(tiles):
                m[top:top + 8, t * LANES:(t + 1) * LANES] = done[k][t]
        below_at = start + size
        if below_at >= bands:
            return
        full = [jnp.concatenate([done[k][t] for k in range(count)], axis=0) for t in range(tiles)]
        kept = list(full)
        row_ids = lax.broadcasted_iota(jnp.int32, (size, LANES), 0) + start % LANES
        lane_ids = lax.broadcasted_iota(jnp.int32, (size, LANES), 1)
        upper = (lane_ids > row_ids) & (lane_ids < start % LANES + size)
        kept[start // LANES] = jnp.where(upper, 0.0, kept[start // LANES])
        splits = [split3(part) for part in kept]
        terms = ((0, 0), (1, 0), (2, 0), (0, 1), (0, 2), (1, 1))
        copies = LANES // size
        depth = -(-len(terms) // copies)
        zero = jnp.zeros((size, LANES), jnp.float32)
        right = jnp.concatenate(
            [jnp.concatenate([splits[t][b] for a, b in terms] + [zero] * (depth * copies - len(terms)), axis=0)
             for t in range(tiles)], axis=1).astype(jnp.bfloat16)
        which = lax.broadcasted_iota(jnp.int32, (LANES, LANES), 1) // size
        for t in range(below_at // LANES, tiles):
            flipped = split3(jnp.transpose(jnp.concatenate([full[t]] * copies, axis=0)))
            pieces = []
            for g in range(depth):
                group = [flipped[a] for a, b in terms[g * copies:(g + 1) * copies]]
                piece = group[0]
                for i in range(1, copies):
                    piece = jnp.where(which == i, group[i] if i < len(group) else 0.0, piece)
                pieces.append(piece)
            left = jnp.concatenate(pieces, axis=1).astype(jnp.bfloat16)
            lo = max(below_at, t * LANES)
            bounds = [lo]
            while bounds[-1] < min(bands, (t + 1) * LANES):
                bounds.append(min(bounds[-1] + SUPER, bands, (t + 1) * LANES))
            for low_row, high_row in zip(bounds[:-1], bounds[1:]):
                update = lax.dot_general(
                    left[low_row - t * LANES:high_row - t * LANES], right, (((1,), (0,)), ((), ())),
                    preferred_element_type=jnp.float32)
                for u in range(tiles):
                    old = m[low_row:high_row, u * LANES:(u + 1) * LANES]
                    if start // LANES == u:
                        lanes = lax.broadcasted_iota(jnp.int32, (high_row - low_row, LANES), 1)
                        old = jnp.where((lanes >= start % LANES) & (lanes < start % LANES + size), 0.0, old)
                    m[low_row:high_row, u * LANES:(u + 1) * LANES] = old - update[:, u * LANES:(u + 1) * LANES]

    h, w = lines // 2, width // 2
    one = h * w
    two = one // 4
    three = two // 4
    base2, base3 = 3 * one, 3 * one + 3 * two
    state = {}

    def stage0():
        rim_wait(pair)
        lift_samples(z1, fl1, fr1, lines, width, first, last, ((v2, 0), (t_ref, 0), (t_ref, one), (t_ref, 2 * one)))
        state["lines"] = line_copy(1, v2, n2, h, w)

    def stage1():
        state["lines"].wait()
        lift_lines(v2, n2, z2, h, w, ln)
        rims(z2, h, w, el2, er2)
        state["pair"] = rim_copies(1, el2, er2, fl2, fr2)

    def stage2():
        rim_wait(state["pair"])
        lift_samples(z2, fl2, fr2, h, w, first, last,
                     ((v3, 0), (t_ref, base2), (t_ref, base2 + two), (t_ref, base2 + 2 * two)))
        state["lines"] = line_copy(2, v3, n3, h // 2, w // 2)

    def stage3():
        state["lines"].wait()
        lift_lines(v3, n3, z3, h // 2, w // 2, ln)
        rims(z3, h // 2, w // 2, el3, er3)
        state["pair"] = rim_copies(2, el3, er3, fl3, fr3)

    def stage4():
        rim_wait(state["pair"])
        lift_samples(z3, fl3, fr3, h // 2, w // 2, first, last,
                     ((t_ref, base3 + 3 * three), (t_ref, base3), (t_ref, base3 + three), (t_ref, base3 + 2 * three)))
        for t in range(tiles):
            top_part = t_ref[t].astype(jnp.bfloat16)
            th[t] = top_part
            tl[t] = (t_ref[t] - top_part.astype(jnp.float32)).astype(jnp.bfloat16)

    def pack(dest, at, lane0, wide_out, low_row, count):
        group = LANES // wide_out
        pieces = [rest[pl.ds(low_row + b, count // group, stride=group), :][:, lane0:lane0 + wide_out]
                  for b in range(group)]
        at = at + low_row // group
        dest[at:at + count // group, :] = jnp.concatenate(pieces, axis=1)

    def final(r):
        low_row = r * LANES
        count = min(LANES, bands - low_row)
        keep = lax.broadcasted_iota(jnp.int32, (count, LANES), 1) <= lax.broadcasted_iota(jnp.int32, (count, LANES), 0)
        parts = [m[low_row:low_row + count, t * LANES:(t + 1) * LANES] for t in range(r + 1)]
        parts[r] = jnp.where(keep, parts[r], 0.0)
        whole = jnp.concatenate(parts, axis=1)
        upper = whole.astype(jnp.bfloat16)
        lower = (whole - upper.astype(jnp.float32)).astype(jnp.bfloat16)
        left = jnp.concatenate([upper, lower, upper], axis=1)
        chunks = t_ref.shape[1] // LANES
        for q in range(0, chunks, 2):
            pix = slice(q * LANES, min(q + 2, chunks) * LANES)
            big = [th[t, pix, :] for t in range(r + 1)]
            small = [tl[t, pix, :] for t in range(r + 1)]
            right = jnp.concatenate(big + big + small, axis=1)
            out = lax.dot_general(left, right, (((1,), (1,)), ((), ())), preferred_element_type=jnp.float32)
            for b in range(out.shape[1] // LANES):
                part = out[:, b * LANES:(b + 1) * LANES]
                if q + b < o1_ref.shape[0]:
                    o1_ref[q + b, low_row:low_row + count, :] = part
                else:
                    rest[low_row:low_row + count, :] = part
        for i in range(3):
            pack(o2_ref, i * (o2_ref.shape[0] // 3), i * two, two, low_row, count)
            pack(o3_ref, i * (o3_ref.shape[0] // 3), 3 * two + i * three, three, low_row, count)
        pack(o4_ref, 0, 3 * two + 3 * three, three, low_row, count)

    stages = [stage0, stage1, stage2, stage3, stage4]
    ready = 0
    for start in range(0, bands, SUPER):
        superblock(start)
        if stages:
            stages.pop(0)()
        if not stages:
            while ready * LANES < bands and min(bands, (ready + 1) * LANES) <= start + SUPER:
                final(ready)
                ready += 1


def store_kernel(*refs):
    count = len(refs) // 2
    copies = [pltpu.make_async_copy(refs[i], refs[count + i], refs[-1].at[i]) for i in range(count)]
    for copy in copies:
        copy.start()
    for copy in copies:
        copy.wait()


def store_call(arrays):
    return pl.pallas_call(
        store_kernel,
        out_shape=tuple(jax.ShapeDtypeStruct(a.shape, a.dtype) for a in arrays),
        in_specs=[pl.BlockSpec(memory_space=pltpu.VMEM)] * len(arrays),
        out_specs=(pl.BlockSpec(memory_space=pl.ANY),) * len(arrays),
        scratch_shapes=[pltpu.SemaphoreType.DMA((len(arrays),))],
        compiler_params=pltpu.CompilerParams(vmem_limit_bytes=4 * 1024 * 1024),
    )(*arrays)


def gram_call(cube, bands, lines, width):
    pixels = lines * width
    samp, line = lax.axis_size("samp"), lax.axis_size("line")
    devices = samp * line
    rows, offsets = blocks_of(bands)
    used = offsets[-1] + rows[-1]
    unit = 8 * devices
    total = -(-used // unit) * unit
    padded = -(-bands // LANES) * LANES
    f32 = jnp.float32
    sem = pltpu.SemaphoreType.DMA
    return pl.pallas_call(
        functools.partial(gram_kernel, samp, line, bands, lines, width),
        out_shape=(jax.ShapeDtypeStruct((3, bands, LANES), f32),
                   jax.ShapeDtypeStruct((3 * bands * (pixels // 16) // LANES, LANES), f32),
                   jax.ShapeDtypeStruct((3 * bands * (pixels // 64) // LANES, LANES), f32),
                   jax.ShapeDtypeStruct((bands * (pixels // 64) // LANES, LANES), f32)),
        in_specs=[pl.BlockSpec(memory_space=pltpu.VMEM)],
        out_specs=(pl.BlockSpec(memory_space=pltpu.VMEM),) * 4,
        scratch_shapes=[
            pltpu.VMEM((padded // LANES, pixels, LANES), f32),
            pltpu.VMEM((padded // LANES, pixels, LANES), jnp.bfloat16),
            pltpu.VMEM((padded // LANES, pixels, LANES), jnp.bfloat16), pltpu.VMEM((bands, padded), f32),
            pltpu.VMEM((bands, LANES), f32), pltpu.VMEM((total, LANES), f32),
            *[pltpu.VMEM((padded // LANES, pixels // 4 ** i, LANES), f32) for i in (0, 1, 2)],
            *[pltpu.VMEM((padded // LANES, pixels // 4 ** i, LANES), f32) for i in (0, 1, 2)],
            *[pltpu.VMEM((padded // LANES, RIM * width // 2 ** i, LANES), f32) for i in (0, 1, 2)],
            *[pltpu.VMEM((padded // LANES, 2 * lines // 2 ** i, LANES), f32) for i in (0, 0, 1, 1, 2, 2)],
            *[pltpu.VMEM((padded // LANES, 2 * lines // 2 ** i, LANES), f32) for i in (0, 0, 1, 1, 2, 2)],
            sem((3,)), sem((3,)), sem((3, 2)), sem((3, 2)),
            pltpu.VMEM((padded, pixels), f32), pltpu.VMEM((1, padded), f32),
            pltpu.VMEM((devices - 1, 1, padded), f32), pltpu.VMEM((total, LANES), f32),
            pltpu.VMEM((line - 1, total // line, LANES), f32),
            pltpu.VMEM((samp - 1, total // devices, LANES), f32), pltpu.VMEM((total, LANES), f32),
            sem((devices - 1,)), sem((devices - 1,)), sem((line - 1,)), sem((line - 1,)),
            sem((samp - 1,)), sem((samp - 1,)), sem((samp - 1,)), sem((samp - 1,)),
            sem((line - 1,)), sem((line - 1,)),
        ],
        compiler_params=pltpu.CompilerParams(collective_id=0, has_side_effects=True,
                                             vmem_limit_bytes=32 * 1024 * 1024),
    )(cube.reshape(-1, LANES))


def local(cube):
    return tuple(out.reshape(-1) for out in store_call(gram_call(cube, BANDS, LD, SD)))


def solution(mesh):
    in_specs = (P(("groups", "samp", "line")),)
    out_specs = (
        P(("groups", "samp", "line")),
        P(("groups", "samp", "line")),
        P(("groups", "samp", "line")),
        P(("groups", "samp", "line")),
    )
    return jax.shard_map(local, mesh=mesh, in_specs=in_specs, out_specs=out_specs, check_vma=False)
```

```python
import functools
import jax
import jax.numpy as jnp
from jax import lax
from jax.experimental import pallas as pl
from jax.experimental.pallas import tpu as pltpu
from jax.sharding import PartitionSpec as P

BANDS = 432
LD = 32
SD = 16

MESH = pl.DeviceIdType.MESH
HIGH = lax.Precision.HIGHEST
LANES = 128
SUPER = 64


def blocks_of(bands):
    rows = [bands - start for start in range(0, bands, LANES)]
    offsets = [sum(rows[:i]) for i in range(len(rows))]
    return rows, offsets


alpha_lift = -1.586134342059924
beta_lift = -0.052980118572961
gamma_lift = 0.882911075530934
delta_lift = 0.443506852043971
scale_lift = 1.230174104914001
RIM = 4


def lift_list(values):
    evens, odds = values[0::2], values[1::2]
    odds = [o + alpha_lift * (e + f) for o, e, f in zip(odds[:-1], evens[:-1], evens[1:])]
    evens = [e + beta_lift * (o + q) for e, o, q in zip(evens[1:-1], odds[:-1], odds[1:])]
    odds = [o + gamma_lift * (e + f) for o, e, f in zip(odds[1:-1], evens[:-1], evens[1:])]
    evens = [e + delta_lift * (o + q) for e, o, q in zip(evens[1:-1], odds[:-1], odds[1:])]
    return [e * (1.0 / scale_lift) for e in evens], [o * scale_lift for o in odds[1:]]


def lift_lines(src, halo, dst, lines, width, ln, centre=None):
    half = lines // 2
    for t in range(src.shape[0]):
        own = [src[t, i * width:(i + 1) * width] for i in range(lines)]
        got = [halo[t, i * width:(i + 1) * width] for i in range(RIM)]
        if centre is not None:
            middle = centre[:, t * LANES:(t + 1) * LANES]
            own = [o - middle for o in own]
            got = [o - middle for o in got]
        before = [jnp.where(ln == 0, own[RIM - i], got[i]) for i in range(RIM)]
        after = [jnp.where(ln == 0, got[i], own[lines - 2 - i]) for i in range(RIM)]
        low, high = lift_list(before + own + after)
        for i in range(half):
            dst[t, i * width:(i + 1) * width] = low[i]
            dst[t, (half + i) * width:(half + i + 1) * width] = high[i]


def rims(z, lines, width, left, right):
    for t in range(z.shape[0]):
        low = [z[t, pl.ds(s, lines, stride=width), :] for s in range(3)]
        top = [z[t, pl.ds(s, lines, stride=width), :] for s in range(width - 4, width)]
        left[t, :lines] = low[0]
        left[t, lines:] = low[0] + beta_lift * (low[1] + alpha_lift * (low[0] + low[2]))
        right[t, :lines] = top[3] + alpha_lift * top[2]
        right[t, lines:] = top[2] + beta_lift * (top[1] + alpha_lift * (top[0] + top[2]))


def lift_samples(z, from_left, from_right, lines, width, first, last, dests):
    half, n = lines // 2, width // 2
    for t in range(z.shape[0]):
        evens = [z[t, pl.ds(2 * i, lines, stride=width), :] for i in range(n)]
        odds = [z[t, pl.ds(2 * i + 1, lines, stride=width), :] for i in range(n)]
        beyond = jnp.where(last, evens[-1], from_right[t, :lines])
        odds1 = [o + alpha_lift * (e + f) for o, e, f in zip(odds, evens, evens[1:] + [beyond])]
        before = jnp.where(first, odds1[0], from_left[t, :lines] + alpha_lift * evens[0])
        evens1 = [e + beta_lift * (p + o) for e, p, o in zip(evens, [before] + odds1[:-1], odds1)]
        beyond = jnp.where(last, evens1[-1], from_right[t, lines:] + beta_lift * odds1[-1])
        odds2 = [o + gamma_lift * (e + f) for o, e, f in zip(odds1, evens1, evens1[1:] + [beyond])]
        outside = from_left[t, lines:] + beta_lift * before
        before = jnp.where(first, odds2[0], before + gamma_lift * (outside + evens1[0]))
        evens2 = [e + delta_lift * (p + o) for e, p, o in zip(evens1, [before] + odds2[:-1], odds2)]
        for i in range(n):
            low, high = evens2[i] * (1.0 / scale_lift), odds2[i] * scale_lift
            for (ref, base), value in zip(dests, (low[:half], low[half:], high[:half], high[half:])):
                ref[t, pl.ds(base + i, half, stride=n), :] = value


def split3(value):
    first = value.astype(jnp.bfloat16).astype(jnp.float32)
    rest = value - first
    second = rest.astype(jnp.bfloat16).astype(jnp.float32)
    return first, second, rest - second


def gram_kernel(samp, line, bands, lines, width, x_ref, o1_ref, o2_ref, o3_ref, o4_ref, t_ref, th, tl, m, rest, corr, v1, v2, v3, z1, z2, z3, n1, n2, n3, el1, er1, el2, er2, el3, er3, fl1, fr1, fl2, fr2, fl3, fr3,
                l_send, l_recv, r_send, r_recv, xs, sums, sums_in, g, half_in,
                chunk_in, tot, s_send, s_recv, h_send, h_recv, c_send, c_recv, a_send, a_recv,
                b_send, b_recv):
    me, ln = lax.axis_index("samp"), lax.axis_index("line")
    devices = samp * line
    pixels = lines * width
    first, last = me == 0, me == samp - 1
    flat = me * line + ln
    packs = pixels // LANES
    padded = xs.shape[0]

    def peer(d):
        other = lax.rem(flat + d, devices)
        return {"samp": other // line, "line": lax.rem(other, line)}

    def line_copy(level, src, dst, tall, wide):
        rows = RIM * wide
        start = pl.multiple_of((1 - ln) * ((tall - RIM) * wide), 8)
        copy = pltpu.make_async_remote_copy(src.at[:, pl.ds(start, rows)], dst, l_send.at[level], l_recv.at[level],
                                            device_id={"line": 1 - ln}, device_id_type=MESH)
        copy.start()
        return copy

    def rim_copies(level, left, right, from_left, from_right):
        below = pltpu.make_async_remote_copy(left, from_right, r_send.at[level, 0], r_recv.at[level, 0],
                                             device_id={"samp": jnp.maximum(me - 1, 0)}, device_id_type=MESH)
        above = pltpu.make_async_remote_copy(right, from_left, r_send.at[level, 1], r_recv.at[level, 1],
                                             device_id={"samp": jnp.minimum(me + 1, samp - 1)}, device_id_type=MESH)

        @pl.when(me > 0)
        def _():
            below.start()

        @pl.when(me < samp - 1)
        def _():
            above.start()

        return below, above

    def rim_wait(pair):
        below, above = pair

        @pl.when(me > 0)
        def _():
            below.wait_send()
            above.wait_recv()

        @pl.when(me < samp - 1)
        def _():
            above.wait_send()
            below.wait_recv()

    for ref in (fl1, fr1, fl2, fr2, fl3, fr3):
        ref[...] = jnp.zeros_like(ref)
    barrier = pltpu.get_barrier_semaphore()
    for d in range(1, devices):
        pl.semaphore_signal(barrier, inc=1, device_id=peer(d), device_id_type=MESH)
    rows, offsets = blocks_of(bands)
    used = offsets[-1] + rows[-1]
    for q in range(packs):
        part = x_ref[pl.ds(q, bands, stride=packs), :]
        xs[0:bands, q * LANES:(q + 1) * LANES] = part
        if padded > bands:
            xs[bands:, q * LANES:(q + 1) * LANES] = jnp.zeros((padded - bands, LANES), jnp.float32)
    for t in range(v1.shape[0]):
        v1[t] = jnp.transpose(xs[t * LANES:(t + 1) * LANES, :])
    folded = xs[:, 0:LANES]
    for q in range(1, packs):
        folded = folded + xs[:, q * LANES:(q + 1) * LANES]
    folded = jnp.concatenate(split3(folded), axis=1).astype(jnp.bfloat16)
    row_sums = lax.dot_general(jnp.ones((8, 3 * LANES), jnp.bfloat16), folded, (((1,), (1,)), ((), ())),
                               preferred_element_type=jnp.float32)[0:1]
    centre = lax.dot_general(folded, jnp.ones((3 * LANES, LANES), jnp.bfloat16), (((1,), (0,)), ((), ())),
                             preferred_element_type=jnp.float32) / float(pixels)
    parts = [xs[:, q * LANES:(q + 1) * LANES] - centre for q in range(packs)]
    energy = parts[0] * parts[0]
    for part in parts[1:]:
        energy = energy + part * part
    energy = jnp.sum(jnp.sum(energy, axis=0, keepdims=True), axis=1, keepdims=True)
    sum_lane = lax.broadcasted_iota(jnp.int32, (1, padded), 1)
    sums[...] = jnp.where(sum_lane < bands, row_sums, energy)
    pl.semaphore_wait(barrier, devices - 1)
    lines1 = line_copy(0, v1, n1, lines, width)
    copies = []
    for d in range(1, devices):
        copy = pltpu.make_async_remote_copy(sums, sums_in.at[d - 1], s_send.at[d - 1], s_recv.at[d - 1],
                                            device_id=peer(d), device_id_type=MESH)
        copy.start()
        copies.append(copy)
    sum_copies = copies
    local_mean = row_sums / float(pixels)
    coarse = [part.astype(jnp.bfloat16) for part in parts]
    fine = [(part - top_part.astype(jnp.float32)).astype(jnp.bfloat16) for part, top_part in zip(parts, coarse)]
    tall = jnp.concatenate(coarse + coarse + fine + fine, axis=1)
    flat_right = jnp.concatenate(coarse + fine + coarse + fine, axis=1)
    part_rows = g.shape[0] // 2
    half = part_rows // line
    chunk = half // samp

    def line_swap(p):
        made = []
        for d in range(1, line):
            other = lax.rem(ln + d, line)
            copy = pltpu.make_async_remote_copy(
                g.at[pl.ds(pl.multiple_of(p * part_rows + other * half, 8), half)], half_in.at[p, d - 1],
                h_send.at[p, d - 1], h_recv.at[p, d - 1], device_id={"line": other}, device_id_type=MESH)
            copy.start()
            made.append(copy)
        return made

    def scatter(p, swaps):
        for copy in swaps:
            copy.wait()
        mine = pl.ds(pl.multiple_of(p * part_rows + ln * half, 8), half)
        value = g[mine, :]
        for d in range(1, line):
            value = value + half_in[p, d - 1]
        g[mine, :] = value
        made = []
        for d in range(1, samp):
            other = lax.rem(me + d, samp)
            copy = pltpu.make_async_remote_copy(
                g.at[pl.ds(pl.multiple_of(p * part_rows + ln * half + other * chunk, 8), chunk)],
                chunk_in.at[p, d - 1], c_send.at[p, d - 1], c_recv.at[p, d - 1],
                device_id={"samp": other}, device_id_type=MESH)
            copy.start()
            made.append(copy)
        return made

    def gather(p, scatters):
        for copy in scatters:
            copy.wait()
        own = pl.ds(pl.multiple_of(p * part_rows + ln * half + me * chunk, 8), chunk)
        value = g[own, :] + corr[own, :]
        for d in range(1, samp):
            value = value + chunk_in[p, d - 1]
        tot[own, :] = value
        made = []
        for d in range(1, samp):
            other = lax.rem(me + d, samp)
            copy = pltpu.make_async_remote_copy(tot.at[own], tot.at[own], a_send.at[p, d - 1], a_recv.at[p, d - 1],
                                                device_id={"samp": other}, device_id_type=MESH)
            copy.start()
            made.append(copy)
        return made

    def line_gather(p, gathers):
        for copy in gathers:
            copy.wait()
        mine = pl.ds(pl.multiple_of(p * part_rows + ln * half, 8), half)
        made = []
        for d in range(1, line):
            other = lax.rem(ln + d, line)
            copy = pltpu.make_async_remote_copy(tot.at[mine], tot.at[mine], b_send.at[p, d - 1], b_recv.at[p, d - 1],
                                                device_id={"line": other}, device_id_type=MESH)
            copy.start()
            made.append(copy)
        return made

    swaps = []
    for q in range(0, len(rows), 2):
        span = min(2 * LANES, padded - q * LANES)
        both = lax.dot_general(tall[q * LANES:bands], flat_right[q * LANES:q * LANES + span],
                               (((1,), (1,)), ((), ())), preferred_element_type=jnp.float32)
        for b in range(span // LANES):
            g[offsets[q + b]:offsets[q + b] + rows[q + b], :] = both[b * LANES:, b * LANES:(b + 1) * LANES]
        if q == 0:
            swaps.append(line_swap(0))
    if g.shape[0] > used:
        g[used:, :] = jnp.zeros((g.shape[0] - used, LANES), jnp.float32)
    swaps.append(line_swap(1))
    lines1.wait()
    lift_lines(v1, n1, z1, lines, width, ln, local_mean)
    rims(z1, lines, width, el1, er1)
    pair = rim_copies(0, el1, er1, fl1, fr1)
    scatters = [scatter(p, swaps[p]) for p in range(2)]
    for copy in sum_copies:
        copy.wait()
    gathered = jnp.concatenate([sums[...]] + [sums_in[d - 1] for d in range(1, devices)], axis=0)
    all_lane = lax.broadcasted_iota(jnp.int32, (devices, padded), 1)
    traces = jnp.sum(gathered[:, padded - 1:padded], axis=0, keepdims=True)
    means = jnp.where(all_lane < bands, gathered, 0.0) / float(pixels)
    mean = jnp.sum(means, axis=0, keepdims=True) / float(devices)
    spread = means - mean
    trace = traces + float(pixels) * jnp.sum(jnp.sum(spread * spread, axis=0, keepdims=True), axis=1, keepdims=True)
    shift = local_mean - mean
    for q, (count, offset) in enumerate(zip(rows, offsets)):
        corr[offset:offset + count, :] = float(pixels) * lax.dot_general(
            spread, spread[:, q * LANES:(q + 1) * LANES], (((0,), (0,)), ((), ())), precision=HIGH,
            preferred_element_type=jnp.float32)[q * LANES:q * LANES + count]
    if g.shape[0] > used:
        corr[used:, :] = jnp.zeros((g.shape[0] - used, LANES), jnp.float32)
    gathers = [gather(p, scatters[p]) for p in range(2)]
    h, w = lines // 2, width // 2
    one = h * w
    two = one // 4
    three = two // 4
    base2, base3 = 3 * one, 3 * one + 3 * two
    rim_wait(pair)
    below_shift = sums_in[line - 1] / float(pixels) - local_mean
    above_shift = sums_in[devices - line - 1] / float(pixels) - local_mean
    inner = 1.0 + beta_lift * (1.0 + 2.0 * alpha_lift)
    for t in range(v1.shape[0]):
        part = slice(t * LANES, (t + 1) * LANES)
        low_half = slice(0, lines // 2)
        next_half = slice(lines, lines + lines // 2)
        fl1[t, low_half] = fl1[t, low_half] + below_shift[:, part] * (1.0 + alpha_lift)
        fl1[t, next_half] = fl1[t, next_half] + below_shift[:, part] * inner
        fr1[t, low_half] = fr1[t, low_half] + above_shift[:, part]
        fr1[t, next_half] = fr1[t, next_half] + above_shift[:, part] * inner
    lift_samples(z1, fl1, fr1, lines, width, first, last, ((v2, 0), (t_ref, 0), (t_ref, one), (t_ref, 2 * one)))
    for t in range(v1.shape[0]):
        v2[t] = v2[t] + shift[:, t * LANES:(t + 1) * LANES]
    lines2 = line_copy(1, v2, n2, h, w)
    closing = line_gather(0, gathers[0])
    lines2.wait()
    lift_lines(v2, n2, z2, h, w, ln)
    rims(z2, h, w, el2, er2)
    pair2 = rim_copies(1, el2, er2, fl2, fr2)
    for copy in closing:
        copy.wait()
    wide = m.shape[1]
    diag = lax.broadcasted_iota(jnp.int32, (LANES, LANES), 0) == lax.broadcasted_iota(
        jnp.int32, (LANES, LANES), 1)
    scale = 1.0 / float(pixels * devices)
    ridge = trace * scale * (0.01 / bands)

    def place(q, fresh):
        offset = offsets[q]
        for b in range(q, len(rows)):
            size = min(LANES, rows[b])
            start = offset + (b - q) * LANES
            block = tot[start:start + size, :] * scale
            row_part, col_part = slice(q * LANES, q * LANES + size), slice(q * LANES, (q + 1) * LANES)
            if b == q:
                low = jnp.where(diag[:size], block + ridge, block)
                m[row_part, col_part] = low if fresh else m[row_part, col_part] + low
            else:
                if size < LANES:
                    block = jnp.concatenate([block, jnp.zeros((LANES - size, LANES), jnp.float32)], axis=0)
                upper_rows, upper_cols = slice(q * LANES, (q + 1) * LANES), slice(b * LANES, (b + 1) * LANES)
                lower_rows = slice(b * LANES, b * LANES + size)
                flipped = jnp.transpose(block)
                if fresh:
                    m[upper_rows, upper_cols] = flipped
                    m[lower_rows, col_part] = block[:size]
                else:
                    m[upper_rows, upper_cols] = m[upper_rows, upper_cols] + flipped
                    m[lower_rows, col_part] = m[lower_rows, col_part] + block[:size]

    place(0, True)
    m[LANES:, LANES:] = jnp.zeros((bands - LANES, wide - LANES), jnp.float32)
    sub = lax.broadcasted_iota(jnp.int32, (8, LANES), 0)
    lane = lax.broadcasted_iota(jnp.int32, (8, LANES), 1)
    tiles = wide // LANES

    def superblock(start):
        size = min(SUPER, bands - start)
        count = size // 8
        panels = [[m[start + 8 * i:start + 8 * i + 8, t * LANES:(t + 1) * LANES] for t in range(tiles)]
                  for i in range(count)]
        done = []

        def spread(tile, lane0):
            return [jnp.broadcast_to(tile[:, lane0 + e:lane0 + e + 1], (8, LANES)) for e in range(8)]

        ahead = spread(panels[0][start // LANES], start % LANES)
        for k in range(count):
            top = start + 8 * k
            at, lane0 = top // LANES, top % LANES
            own = panels[k]
            cols = ahead
            if k + 1 < count:
                ahead = spread(panels[k + 1][(top + 8) // LANES], (top + 8) % LANES)
            later = range(k + 1, count)
            below = {p: [jnp.broadcast_to(panels[p][at][:, lane0 + e:lane0 + e + 1], (8, LANES)) for e in range(8)]
                     for p in later}
            inside = (lane >= lane0) & (lane < lane0 + 8)
            own[at] = jnp.where(inside, jnp.where(lane - lane0 == sub, 1.0, 0.0), own[at])
            for p in later:
                panels[p][at] = jnp.where(inside, 0.0, panels[p][at])
            pivots = None
            for b in range(8):
                pivot = jnp.broadcast_to(cols[b][b:b + 1, :], (8, LANES))
                inverse = 1.0 / pivot
                pivots = pivot if pivots is None else jnp.where(sub == b, pivot, pivots)
                factor = jnp.where(sub > b, cols[b] * inverse, 0.0)
                rows_b = [jnp.broadcast_to(own[t][b:b + 1, :], (8, LANES)) for t in range(tiles)]
                heads = {e: jnp.broadcast_to(cols[e][b:b + 1, :], (8, LANES)) for e in range(b + 1, 8)}
                for e in range(b + 1, 8):
                    cols[e] = cols[e] - factor * heads[e]
                for p in later:
                    scaled = below[p][b] * inverse
                    if p == k + 1:
                        ahead = [ahead[e] - scaled * jnp.broadcast_to(below[p][b][e:e + 1, :], (8, LANES))
                                 for e in range(8)]
                    for e in range(b + 1, 8):
                        below[p][e] = below[p][e] - scaled * heads[e]
                    for t in range(tiles):
                        panels[p][t] = panels[p][t] - scaled * rows_b[t]
                if b < 7:
                    for t in range(tiles):
                        own[t] = own[t] - factor * rows_b[t]
            root = lax.rsqrt(pivots)
            done.append([own[t] * root for t in range(tiles)])
            for t in range(tiles):
                m[top:top + 8, t * LANES:(t + 1) * LANES] = done[k][t]
        below_at = start + size
        if below_at >= bands:
            return
        full = [jnp.concatenate([done[k][t] for k in range(count)], axis=0) for t in range(tiles)]
        kept = list(full)
        row_ids = lax.broadcasted_iota(jnp.int32, (size, LANES), 0) + start % LANES
        lane_ids = lax.broadcasted_iota(jnp.int32, (size, LANES), 1)
        upper = (lane_ids > row_ids) & (lane_ids < start % LANES + size)
        kept[start // LANES] = jnp.where(upper, 0.0, kept[start // LANES])
        splits = [split3(part) for part in kept]
        terms = ((0, 0), (1, 0), (2, 0), (0, 1), (0, 2), (1, 1))
        copies = LANES // size
        depth = -(-len(terms) // copies)
        zero = jnp.zeros((size, LANES), jnp.float32)
        right = jnp.concatenate(
            [jnp.concatenate([splits[t][b] for a, b in terms] + [zero] * (depth * copies - len(terms)), axis=0)
             for t in range(tiles)], axis=1).astype(jnp.bfloat16)
        which = lax.broadcasted_iota(jnp.int32, (LANES, LANES), 1) // size
        for t in range(below_at // LANES, tiles):
            flipped = split3(jnp.transpose(jnp.concatenate([full[t]] * copies, axis=0)))
            pieces = []
            for g in range(depth):
                group = [flipped[a] for a, b in terms[g * copies:(g + 1) * copies]]
                piece = group[0]
                for i in range(1, copies):
                    piece = jnp.where(which == i, group[i] if i < len(group) else 0.0, piece)
                pieces.append(piece)
            left = jnp.concatenate(pieces, axis=1).astype(jnp.bfloat16)
            lo = max(below_at, t * LANES)
            bounds = [lo]
            while bounds[-1] < min(bands, (t + 1) * LANES):
                bounds.append(min(bounds[-1] + SUPER, bands, (t + 1) * LANES))
            for low_row, high_row in zip(bounds[:-1], bounds[1:]):
                update = lax.dot_general(
                    left[low_row - t * LANES:high_row - t * LANES], right, (((1,), (0,)), ((), ())),
                    preferred_element_type=jnp.float32)
                for u in range(tiles):
                    old = m[low_row:high_row, u * LANES:(u + 1) * LANES]
                    if start // LANES == u:
                        lanes = lax.broadcasted_iota(jnp.int32, (high_row - low_row, LANES), 1)
                        old = jnp.where((lanes >= start % LANES) & (lanes < start % LANES + size), 0.0, old)
                    m[low_row:high_row, u * LANES:(u + 1) * LANES] = old - update[:, u * LANES:(u + 1) * LANES]

    state = {}

    def stage_rest():
        closing = line_gather(1, gathers[1])
        rim_wait(pair2)
        lift_samples(z2, fl2, fr2, h, w, first, last,
                     ((v3, 0), (t_ref, base2), (t_ref, base2 + two), (t_ref, base2 + 2 * two)))
        state["lines"] = line_copy(2, v3, n3, h // 2, w // 2)
        for copy in closing:
            copy.wait()
        for q in range(1, len(rows)):
            place(q, False)

    def stage0():
        state["lines"].wait()
        lift_lines(v3, n3, z3, h // 2, w // 2, ln)
        rims(z3, h // 2, w // 2, el3, er3)
        state["pair"] = rim_copies(2, el3, er3, fl3, fr3)

    def stage1():
        rim_wait(state["pair"])
        lift_samples(z3, fl3, fr3, h // 2, w // 2, first, last,
                     ((t_ref, base3 + 3 * three), (t_ref, base3), (t_ref, base3 + three), (t_ref, base3 + 2 * three)))
        for t in range(tiles):
            top_part = t_ref[t].astype(jnp.bfloat16)
            th[t] = top_part
            tl[t] = (t_ref[t] - top_part.astype(jnp.float32)).astype(jnp.bfloat16)

    def pack(dest, at, lane0, wide_out, low_row, count):
        group = LANES // wide_out
        pieces = [rest[pl.ds(low_row + b, count // group, stride=group), :][:, lane0:lane0 + wide_out]
                  for b in range(group)]
        at = at + low_row // group
        dest[at:at + count // group, :] = jnp.concatenate(pieces, axis=1)

    def final(r):
        low_row = r * LANES
        count = min(LANES, bands - low_row)
        keep = lax.broadcasted_iota(jnp.int32, (count, LANES), 1) <= lax.broadcasted_iota(jnp.int32, (count, LANES), 0)
        parts = [m[low_row:low_row + count, t * LANES:(t + 1) * LANES] for t in range(r + 1)]
        parts[r] = jnp.where(keep, parts[r], 0.0)
        whole = jnp.concatenate(parts, axis=1)
        upper = whole.astype(jnp.bfloat16)
        lower = (whole - upper.astype(jnp.float32)).astype(jnp.bfloat16)
        left = jnp.concatenate([upper, lower, upper], axis=1)
        chunks = t_ref.shape[1] // LANES
        for q in range(0, chunks, 2):
            pix = slice(q * LANES, min(q + 2, chunks) * LANES)
            big = [th[t, pix, :] for t in range(r + 1)]
            small = [tl[t, pix, :] for t in range(r + 1)]
            right = jnp.concatenate(big + big + small, axis=1)
            out = lax.dot_general(left, right, (((1,), (1,)), ((), ())), preferred_element_type=jnp.float32)
            for b in range(out.shape[1] // LANES):
                part = out[:, b * LANES:(b + 1) * LANES]
                if q + b < o1_ref.shape[0]:
                    o1_ref[q + b, low_row:low_row + count, :] = part
                else:
                    rest[low_row:low_row + count, :] = part
        for i in range(3):
            pack(o2_ref, i * (o2_ref.shape[0] // 3), i * two, two, low_row, count)
            pack(o3_ref, i * (o3_ref.shape[0] // 3), 3 * two + i * three, three, low_row, count)
        pack(o4_ref, 0, 3 * two + 3 * three, three, low_row, count)

    stages = {LANES // SUPER - 1: stage_rest, LANES // SUPER: stage0, LANES // SUPER + 2: stage1}
    ready = 0
    for start in range(0, bands, SUPER):
        superblock(start)
        if start // SUPER in stages:
            stages.pop(start // SUPER)()
        if not stages:
            while ready * LANES < bands and min(bands, (ready + 1) * LANES) <= start + SUPER:
                final(ready)
                ready += 1


def store_kernel(*refs):
    count = len(refs) // 2
    copies = [pltpu.make_async_copy(refs[i], refs[count + i], refs[-1].at[i]) for i in range(count)]
    for copy in copies:
        copy.start()
    for copy in copies:
        copy.wait()


def store_call(arrays):
    return pl.pallas_call(
        store_kernel,
        out_shape=tuple(jax.ShapeDtypeStruct(a.shape, a.dtype) for a in arrays),
        in_specs=[pl.BlockSpec(memory_space=pltpu.VMEM)] * len(arrays),
        out_specs=(pl.BlockSpec(memory_space=pl.ANY),) * len(arrays),
        scratch_shapes=[pltpu.SemaphoreType.DMA((len(arrays),))],
        compiler_params=pltpu.CompilerParams(vmem_limit_bytes=4 * 1024 * 1024),
    )(*arrays)


def gram_call(cube, bands, lines, width):
    pixels = lines * width
    samp, line = lax.axis_size("samp"), lax.axis_size("line")
    devices = samp * line
    rows, offsets = blocks_of(bands)
    used = offsets[-1] + rows[-1]
    unit = 16 * devices
    total = -(-used // unit) * unit
    padded = -(-bands // LANES) * LANES
    f32 = jnp.float32
    sem = pltpu.SemaphoreType.DMA
    return pl.pallas_call(
        functools.partial(gram_kernel, samp, line, bands, lines, width),
        out_shape=(jax.ShapeDtypeStruct((3, bands, LANES), f32),
                   jax.ShapeDtypeStruct((3 * bands * (pixels // 16) // LANES, LANES), f32),
                   jax.ShapeDtypeStruct((3 * bands * (pixels // 64) // LANES, LANES), f32),
                   jax.ShapeDtypeStruct((bands * (pixels // 64) // LANES, LANES), f32)),
        in_specs=[pl.BlockSpec(memory_space=pltpu.VMEM)],
        out_specs=(pl.BlockSpec(memory_space=pltpu.VMEM),) * 4,
        scratch_shapes=[
            pltpu.VMEM((padded // LANES, pixels, LANES), f32),
            pltpu.VMEM((padded // LANES, pixels, LANES), jnp.bfloat16),
            pltpu.VMEM((padded // LANES, pixels, LANES), jnp.bfloat16), pltpu.VMEM((bands, padded), f32),
            pltpu.VMEM((bands, LANES), f32), pltpu.VMEM((total, LANES), f32),
            *[pltpu.VMEM((padded // LANES, pixels // 4 ** i, LANES), f32) for i in (0, 1, 2)],
            *[pltpu.VMEM((padded // LANES, pixels // 4 ** i, LANES), f32) for i in (0, 1, 2)],
            *[pltpu.VMEM((padded // LANES, RIM * width // 2 ** i, LANES), f32) for i in (0, 1, 2)],
            *[pltpu.VMEM((padded // LANES, 2 * lines // 2 ** i, LANES), f32) for i in (0, 0, 1, 1, 2, 2)],
            *[pltpu.VMEM((padded // LANES, 2 * lines // 2 ** i, LANES), f32) for i in (0, 0, 1, 1, 2, 2)],
            sem((3,)), sem((3,)), sem((3, 2)), sem((3, 2)),
            pltpu.VMEM((padded, pixels), f32), pltpu.VMEM((1, padded), f32),
            pltpu.VMEM((devices - 1, 1, padded), f32), pltpu.VMEM((total, LANES), f32),
            pltpu.VMEM((2, line - 1, total // 2 // line, LANES), f32),
            pltpu.VMEM((2, samp - 1, total // 2 // devices, LANES), f32), pltpu.VMEM((total, LANES), f32),
            sem((devices - 1,)), sem((devices - 1,)), sem((2, line - 1)), sem((2, line - 1)),
            sem((2, samp - 1)), sem((2, samp - 1)), sem((2, samp - 1)), sem((2, samp - 1)),
            sem((2, line - 1)), sem((2, line - 1)),
        ],
        compiler_params=pltpu.CompilerParams(collective_id=0, has_side_effects=True,
                                             vmem_limit_bytes=32 * 1024 * 1024),
    )(cube.reshape(-1, LANES))


def local(cube):
    return tuple(out.reshape(-1) for out in store_call(gram_call(cube, BANDS, LD, SD)))


def solution(mesh):
    in_specs = (P(("groups", "samp", "line")),)
    out_specs = (
        P(("groups", "samp", "line")),
        P(("groups", "samp", "line")),
        P(("groups", "samp", "line")),
        P(("groups", "samp", "line")),
    )
    return jax.shard_map(local, mesh=mesh, in_specs=in_specs, out_specs=out_specs, check_vma=False)
```

```python
import functools
import jax
import jax.numpy as jnp
from jax import lax
from jax.experimental import pallas as pl
from jax.experimental.pallas import tpu as pltpu
from jax.sharding import PartitionSpec as P

BANDS = 432
LD = 32
SD = 16

MESH = pl.DeviceIdType.MESH
HIGH = lax.Precision.HIGHEST
LANES = 128
SUPER = 64
CSTAGE = 3


def blocks_of(bands):
    rows = [bands - start for start in range(0, bands, LANES)]
    offsets = [sum(rows[:i]) for i in range(len(rows))]
    return rows, offsets


alpha_lift = -1.586134342059924
beta_lift = -0.052980118572961
gamma_lift = 0.882911075530934
delta_lift = 0.443506852043971
scale_lift = 1.230174104914001
RIM = 4


def lift_list(values):
    evens, odds = values[0::2], values[1::2]
    odds = [o + alpha_lift * (e + f) for o, e, f in zip(odds[:-1], evens[:-1], evens[1:])]
    evens = [e + beta_lift * (o + q) for e, o, q in zip(evens[1:-1], odds[:-1], odds[1:])]
    odds = [o + gamma_lift * (e + f) for o, e, f in zip(odds[1:-1], evens[:-1], evens[1:])]
    evens = [e + delta_lift * (o + q) for e, o, q in zip(evens[1:-1], odds[:-1], odds[1:])]
    return [e * (1.0 / scale_lift) for e in evens], [o * scale_lift for o in odds[1:]]


def lift_lines(src, halo, dst, lines, width, ln, centre=None):
    half = lines // 2
    for t in range(src.shape[0]):
        own = [src[t, i * width:(i + 1) * width] for i in range(lines)]
        got = [halo[t, i * width:(i + 1) * width] for i in range(RIM)]
        if centre is not None:
            middle = centre[:, t * LANES:(t + 1) * LANES]
            own = [o - middle for o in own]
            got = [o - middle for o in got]
        before = [jnp.where(ln == 0, own[RIM - i], got[i]) for i in range(RIM)]
        after = [jnp.where(ln == 0, got[i], own[lines - 2 - i]) for i in range(RIM)]
        low, high = lift_list(before + own + after)
        for i in range(half):
            dst[t, i * width:(i + 1) * width] = low[i]
            dst[t, (half + i) * width:(half + i + 1) * width] = high[i]


def rims(z, lines, width, left, right):
    for t in range(z.shape[0]):
        low = [z[t, pl.ds(s, lines, stride=width), :] for s in range(3)]
        top = [z[t, pl.ds(s, lines, stride=width), :] for s in range(width - 4, width)]
        left[t, :lines] = low[0]
        left[t, lines:] = low[0] + beta_lift * (low[1] + alpha_lift * (low[0] + low[2]))
        right[t, :lines] = top[3] + alpha_lift * top[2]
        right[t, lines:] = top[2] + beta_lift * (top[1] + alpha_lift * (top[0] + top[2]))


def lift_samples(z, from_left, from_right, lines, width, first, last, dests):
    half, n = lines // 2, width // 2
    for t in range(z.shape[0]):
        evens = [z[t, pl.ds(2 * i, lines, stride=width), :] for i in range(n)]
        odds = [z[t, pl.ds(2 * i + 1, lines, stride=width), :] for i in range(n)]
        beyond = jnp.where(last, evens[-1], from_right[t, :lines])
        odds1 = [o + alpha_lift * (e + f) for o, e, f in zip(odds, evens, evens[1:] + [beyond])]
        before = jnp.where(first, odds1[0], from_left[t, :lines] + alpha_lift * evens[0])
        evens1 = [e + beta_lift * (p + o) for e, p, o in zip(evens, [before] + odds1[:-1], odds1)]
        beyond = jnp.where(last, evens1[-1], from_right[t, lines:] + beta_lift * odds1[-1])
        odds2 = [o + gamma_lift * (e + f) for o, e, f in zip(odds1, evens1, evens1[1:] + [beyond])]
        outside = from_left[t, lines:] + beta_lift * before
        before = jnp.where(first, odds2[0], before + gamma_lift * (outside + evens1[0]))
        evens2 = [e + delta_lift * (p + o) for e, p, o in zip(evens1, [before] + odds2[:-1], odds2)]
        for i in range(n):
            low, high = evens2[i] * (1.0 / scale_lift), odds2[i] * scale_lift
            for (ref, base), value in zip(dests, (low[:half], low[half:], high[:half], high[half:])):
                ref[t, pl.ds(base + i, half, stride=n), :] = value


def split3(value):
    first = value.astype(jnp.bfloat16).astype(jnp.float32)
    rest = value - first
    second = rest.astype(jnp.bfloat16).astype(jnp.float32)
    return first, second, rest - second


def gram_kernel(samp, line, bands, lines, width, x_ref, o1_ref, o2_ref, o3_ref, o4_ref, t_ref, th, tl, m, rest, corr, v1, v2, v3, z1, z2, z3, n1, n2, n3, el1, er1, el2, er2, el3, er3, fl1, fr1, fl2, fr2, fl3, fr3,
                l_send, l_recv, r_send, r_recv, xs, sums, sums_in, g, half_in,
                chunk_in, tot, s_send, s_recv, h_send, h_recv, c_send, c_recv, a_send, a_recv,
                b_send, b_recv):
    me, ln = lax.axis_index("samp"), lax.axis_index("line")
    devices = samp * line
    pixels = lines * width
    first, last = me == 0, me == samp - 1
    flat = me * line + ln
    packs = pixels // LANES
    padded = xs.shape[0]

    def peer(d):
        other = lax.rem(flat + d, devices)
        return {"samp": other // line, "line": lax.rem(other, line)}

    def line_copy(level, src, dst, tall, wide):
        rows = RIM * wide
        start = pl.multiple_of((1 - ln) * ((tall - RIM) * wide), 8)
        copy = pltpu.make_async_remote_copy(src.at[:, pl.ds(start, rows)], dst, l_send.at[level], l_recv.at[level],
                                            device_id={"line": 1 - ln}, device_id_type=MESH)
        copy.start()
        return copy

    def rim_copies(level, left, right, from_left, from_right):
        below = pltpu.make_async_remote_copy(left, from_right, r_send.at[level, 0], r_recv.at[level, 0],
                                             device_id={"samp": jnp.maximum(me - 1, 0)}, device_id_type=MESH)
        above = pltpu.make_async_remote_copy(right, from_left, r_send.at[level, 1], r_recv.at[level, 1],
                                             device_id={"samp": jnp.minimum(me + 1, samp - 1)}, device_id_type=MESH)

        @pl.when(me > 0)
        def _():
            below.start()

        @pl.when(me < samp - 1)
        def _():
            above.start()

        return below, above

    def rim_wait(pair):
        below, above = pair

        @pl.when(me > 0)
        def _():
            below.wait_send()
            above.wait_recv()

        @pl.when(me < samp - 1)
        def _():
            above.wait_send()
            below.wait_recv()

    for ref in (fl1, fr1, fl2, fr2, fl3, fr3):
        ref[...] = jnp.zeros_like(ref)
    barrier = pltpu.get_barrier_semaphore()
    for d in range(1, devices):
        pl.semaphore_signal(barrier, inc=1, device_id=peer(d), device_id_type=MESH)
    rows, offsets = blocks_of(bands)
    used = offsets[-1] + rows[-1]
    for q in range(packs):
        part = x_ref[pl.ds(q, bands, stride=packs), :]
        xs[0:bands, q * LANES:(q + 1) * LANES] = part
        if padded > bands:
            xs[bands:, q * LANES:(q + 1) * LANES] = jnp.zeros((padded - bands, LANES), jnp.float32)
    for t in range(v1.shape[0]):
        v1[t] = jnp.transpose(xs[t * LANES:(t + 1) * LANES, :])
    folded = xs[:, 0:LANES]
    for q in range(1, packs):
        folded = folded + xs[:, q * LANES:(q + 1) * LANES]
    folded = jnp.concatenate(split3(folded), axis=1).astype(jnp.bfloat16)
    row_sums = lax.dot_general(jnp.ones((8, 3 * LANES), jnp.bfloat16), folded, (((1,), (1,)), ((), ())),
                               preferred_element_type=jnp.float32)[0:1]
    centre = lax.dot_general(folded, jnp.ones((3 * LANES, LANES), jnp.bfloat16), (((1,), (0,)), ((), ())),
                             preferred_element_type=jnp.float32) / float(pixels)
    parts = [xs[:, q * LANES:(q + 1) * LANES] - centre for q in range(packs)]
    energy = parts[0] * parts[0]
    for part in parts[1:]:
        energy = energy + part * part
    energy = jnp.sum(jnp.sum(energy, axis=0, keepdims=True), axis=1, keepdims=True)
    sum_lane = lax.broadcasted_iota(jnp.int32, (1, padded), 1)
    sums[...] = jnp.where(sum_lane < bands, row_sums, energy)
    local_mean = row_sums / float(pixels)
    coarse = [part.astype(jnp.bfloat16) for part in parts]
    fine = [(part - top_part.astype(jnp.float32)).astype(jnp.bfloat16) for part, top_part in zip(parts, coarse)]
    tall = jnp.concatenate(coarse + coarse + fine + fine, axis=1)
    flat_right = jnp.concatenate(coarse + fine + coarse + fine, axis=1)
    part_rows = g.shape[0] // 2
    half = part_rows // line
    chunk = half // samp

    def line_swap(p):
        made = []
        for d in range(1, line):
            other = lax.rem(ln + d, line)
            copy = pltpu.make_async_remote_copy(
                g.at[pl.ds(pl.multiple_of(p * part_rows + other * half, 8), half)], half_in.at[p, d - 1],
                h_send.at[p, d - 1], h_recv.at[p, d - 1], device_id={"line": other}, device_id_type=MESH)
            copy.start()
            made.append(copy)
        return made

    def scatter(p, swaps):
        for copy in swaps:
            copy.wait()
        mine = pl.ds(pl.multiple_of(p * part_rows + ln * half, 8), half)
        value = g[mine, :]
        for d in range(1, line):
            value = value + half_in[p, d - 1]
        g[mine, :] = value
        made = []
        for d in range(1, samp):
            other = lax.rem(me + d, samp)
            copy = pltpu.make_async_remote_copy(
                g.at[pl.ds(pl.multiple_of(p * part_rows + ln * half + other * chunk, 8), chunk)],
                chunk_in.at[p, d - 1], c_send.at[p, d - 1], c_recv.at[p, d - 1],
                device_id={"samp": other}, device_id_type=MESH)
            copy.start()
            made.append(copy)
        return made

    def gather(p, scatters):
        for copy in scatters:
            copy.wait()
        own = pl.ds(pl.multiple_of(p * part_rows + ln * half + me * chunk, 8), chunk)
        value = g[own, :] + corr[own, :]
        for d in range(1, samp):
            value = value + chunk_in[p, d - 1]
        tot[own, :] = value
        made = []
        for d in range(1, samp):
            other = lax.rem(me + d, samp)
            copy = pltpu.make_async_remote_copy(tot.at[own], tot.at[own], a_send.at[p, d - 1], a_recv.at[p, d - 1],
                                                device_id={"samp": other}, device_id_type=MESH)
            copy.start()
            made.append(copy)
        return made

    def line_gather(p, gathers):
        for copy in gathers:
            copy.wait()
        mine = pl.ds(pl.multiple_of(p * part_rows + ln * half, 8), half)
        made = []
        for d in range(1, line):
            other = lax.rem(ln + d, line)
            copy = pltpu.make_async_remote_copy(tot.at[mine], tot.at[mine], b_send.at[p, d - 1], b_recv.at[p, d - 1],
                                                device_id={"line": other}, device_id_type=MESH)
            copy.start()
            made.append(copy)
        return made

    for q in range(0, len(rows), 2):
        span = min(2 * LANES, padded - q * LANES)
        both = lax.dot_general(tall[q * LANES:bands], flat_right[q * LANES:q * LANES + span],
                               (((1,), (1,)), ((), ())), preferred_element_type=jnp.float32)
        for b in range(span // LANES):
            g[offsets[q + b]:offsets[q + b] + rows[q + b], :] = both[b * LANES:, b * LANES:(b + 1) * LANES]
    if g.shape[0] > used:
        g[used:, :] = jnp.zeros((g.shape[0] - used, LANES), jnp.float32)
    pl.semaphore_wait(barrier, devices - 1)
    copies = []
    for d in range(1, devices):
        copy = pltpu.make_async_remote_copy(sums, sums_in.at[d - 1], s_send.at[d - 1], s_recv.at[d - 1],
                                            device_id=peer(d), device_id_type=MESH)
        copy.start()
        copies.append(copy)
    sum_copies = copies
    swaps = [line_swap(0)]
    lines1 = line_copy(0, v1, n1, lines, width)
    swaps.append(line_swap(1))
    scatters = [scatter(p, swaps[p]) for p in range(2)]
    lines1.wait()
    lift_lines(v1, n1, z1, lines, width, ln, local_mean)
    rims(z1, lines, width, el1, er1)
    for copy in sum_copies:
        copy.wait()
    gathered = jnp.concatenate([sums[...]] + [sums_in[d - 1] for d in range(1, devices)], axis=0)
    all_lane = lax.broadcasted_iota(jnp.int32, (devices, padded), 1)
    traces = jnp.sum(gathered[:, padded - 1:padded], axis=0, keepdims=True)
    means = jnp.where(all_lane < bands, gathered, 0.0) / float(pixels)
    mean = jnp.sum(means, axis=0, keepdims=True) / float(devices)
    spread = means - mean
    trace = traces + float(pixels) * jnp.sum(jnp.sum(spread * spread, axis=0, keepdims=True), axis=1, keepdims=True)
    shift = local_mean - mean
    for q, (count, offset) in enumerate(zip(rows, offsets)):
        corr[offset:offset + count, :] = float(pixels) * lax.dot_general(
            spread, spread[:, q * LANES:(q + 1) * LANES], (((0,), (0,)), ((), ())), precision=HIGH,
            preferred_element_type=jnp.float32)[q * LANES:q * LANES + count]
    if g.shape[0] > used:
        corr[used:, :] = jnp.zeros((g.shape[0] - used, LANES), jnp.float32)
    gathers = [gather(0, scatters[0])]
    pair = rim_copies(0, el1, er1, fl1, fr1)
    gathers.append(gather(1, scatters[1]))
    h, w = lines // 2, width // 2
    one = h * w
    two = one // 4
    three = two // 4
    base2, base3 = 3 * one, 3 * one + 3 * two
    closing = line_gather(0, gathers[0])
    for copy in closing:
        copy.wait()
    wide = m.shape[1]
    diag = lax.broadcasted_iota(jnp.int32, (LANES, LANES), 0) == lax.broadcasted_iota(
        jnp.int32, (LANES, LANES), 1)
    scale = 1.0 / float(pixels * devices)
    ridge = trace * scale * (0.01 / bands)

    def place(q, fresh):
        offset = offsets[q]
        for b in range(q, len(rows)):
            size = min(LANES, rows[b])
            start = offset + (b - q) * LANES
            block = tot[start:start + size, :] * scale
            row_part, col_part = slice(q * LANES, q * LANES + size), slice(q * LANES, (q + 1) * LANES)
            if b == q:
                low = jnp.where(diag[:size], block + ridge, block)
                m[row_part, col_part] = low if fresh else m[row_part, col_part] + low
            else:
                if size < LANES:
                    block = jnp.concatenate([block, jnp.zeros((LANES - size, LANES), jnp.float32)], axis=0)
                upper_rows, upper_cols = slice(q * LANES, (q + 1) * LANES), slice(b * LANES, (b + 1) * LANES)
                lower_rows = slice(b * LANES, b * LANES + size)
                flipped = jnp.transpose(block)
                if fresh:
                    m[upper_rows, upper_cols] = flipped
                    m[lower_rows, col_part] = block[:size]
                else:
                    m[upper_rows, upper_cols] = m[upper_rows, upper_cols] + flipped
                    m[lower_rows, col_part] = m[lower_rows, col_part] + block[:size]

    place(0, True)
    m[LANES:, LANES:] = jnp.zeros((bands - LANES, wide - LANES), jnp.float32)
    sub = lax.broadcasted_iota(jnp.int32, (8, LANES), 0)
    lane = lax.broadcasted_iota(jnp.int32, (8, LANES), 1)
    tiles = wide // LANES

    def superblock(start):
        size = min(SUPER, bands - start)
        count = size // 8
        panels = [[m[start + 8 * i:start + 8 * i + 8, t * LANES:(t + 1) * LANES] for t in range(tiles)]
                  for i in range(count)]
        done = []

        def spread(tile, lane0):
            return [jnp.broadcast_to(tile[:, lane0 + e:lane0 + e + 1], (8, LANES)) for e in range(8)]

        ahead = spread(panels[0][start // LANES], start % LANES)
        for k in range(count):
            top = start + 8 * k
            at, lane0 = top // LANES, top % LANES
            own = panels[k]
            cols = ahead
            if k + 1 < count:
                ahead = spread(panels[k + 1][(top + 8) // LANES], (top + 8) % LANES)
            later = range(k + 1, count)
            below = {p: [jnp.broadcast_to(panels[p][at][:, lane0 + e:lane0 + e + 1], (8, LANES)) for e in range(8)]
                     for p in later}
            inside = (lane >= lane0) & (lane < lane0 + 8)
            own[at] = jnp.where(inside, jnp.where(lane - lane0 == sub, 1.0, 0.0), own[at])
            for p in later:
                panels[p][at] = jnp.where(inside, 0.0, panels[p][at])
            pivots = None
            for b in range(8):
                pivot = jnp.broadcast_to(cols[b][b:b + 1, :], (8, LANES))
                inverse = 1.0 / pivot
                pivots = pivot if pivots is None else jnp.where(sub == b, pivot, pivots)
                factor = jnp.where(sub > b, cols[b] * inverse, 0.0)
                rows_b = [jnp.broadcast_to(own[t][b:b + 1, :], (8, LANES)) for t in range(tiles)]
                heads = {e: jnp.broadcast_to(cols[e][b:b + 1, :], (8, LANES)) for e in range(b + 1, 8)}
                for e in range(b + 1, 8):
                    cols[e] = cols[e] - factor * heads[e]
                for p in later:
                    scaled = below[p][b] * inverse
                    if p == k + 1:
                        ahead = [ahead[e] - scaled * jnp.broadcast_to(below[p][b][e:e + 1, :], (8, LANES))
                                 for e in range(8)]
                    for e in range(b + 1, 8):
                        below[p][e] = below[p][e] - scaled * heads[e]
                    for t in range(tiles):
                        panels[p][t] = panels[p][t] - scaled * rows_b[t]
                if b < 7:
                    for t in range(tiles):
                        own[t] = own[t] - factor * rows_b[t]
            root = lax.rsqrt(pivots)
            done.append([own[t] * root for t in range(tiles)])
            for t in range(tiles):
                m[top:top + 8, t * LANES:(t + 1) * LANES] = done[k][t]
        below_at = start + size
        if below_at >= bands:
            return
        full = [jnp.concatenate([done[k][t] for k in range(count)], axis=0) for t in range(tiles)]
        kept = list(full)
        row_ids = lax.broadcasted_iota(jnp.int32, (size, LANES), 0) + start % LANES
        lane_ids = lax.broadcasted_iota(jnp.int32, (size, LANES), 1)
        upper = (lane_ids > row_ids) & (lane_ids < start % LANES + size)
        kept[start // LANES] = jnp.where(upper, 0.0, kept[start // LANES])
        splits = [split3(part) for part in kept]
        terms = ((0, 0), (1, 0), (2, 0), (0, 1), (0, 2), (1, 1))
        copies = LANES // size
        depth = -(-len(terms) // copies)
        zero = jnp.zeros((size, LANES), jnp.float32)
        right = jnp.concatenate(
            [jnp.concatenate([splits[t][b] for a, b in terms] + [zero] * (depth * copies - len(terms)), axis=0)
             for t in range(tiles)], axis=1).astype(jnp.bfloat16)
        which = lax.broadcasted_iota(jnp.int32, (LANES, LANES), 1) // size
        for t in range(below_at // LANES, tiles):
            flipped = split3(jnp.transpose(jnp.concatenate([full[t]] * copies, axis=0)))
            pieces = []
            for g in range(depth):
                group = [flipped[a] for a, b in terms[g * copies:(g + 1) * copies]]
                piece = group[0]
                for i in range(1, copies):
                    piece = jnp.where(which == i, group[i] if i < len(group) else 0.0, piece)
                pieces.append(piece)
            left = jnp.concatenate(pieces, axis=1).astype(jnp.bfloat16)
            lo = max(below_at, t * LANES)
            bounds = [lo]
            while bounds[-1] < min(bands, (t + 1) * LANES):
                bounds.append(min(bounds[-1] + SUPER, bands, (t + 1) * LANES))
            for low_row, high_row in zip(bounds[:-1], bounds[1:]):
                update = lax.dot_general(
                    left[low_row - t * LANES:high_row - t * LANES], right, (((1,), (0,)), ((), ())),
                    preferred_element_type=jnp.float32)
                for u in range(tiles):
                    old = m[low_row:high_row, u * LANES:(u + 1) * LANES]
                    if start // LANES == u:
                        lanes = lax.broadcasted_iota(jnp.int32, (high_row - low_row, LANES), 1)
                        old = jnp.where((lanes >= start % LANES) & (lanes < start % LANES + size), 0.0, old)
                    m[low_row:high_row, u * LANES:(u + 1) * LANES] = old - update[:, u * LANES:(u + 1) * LANES]

    state = {}

    def convert(low_pix, high_pix):
        for t in range(tiles):
            top_part = t_ref[t, low_pix:high_pix].astype(jnp.bfloat16)
            th[t, low_pix:high_pix] = top_part
            tl[t, low_pix:high_pix] = (t_ref[t, low_pix:high_pix] - top_part.astype(jnp.float32)).astype(jnp.bfloat16)

    def stage_a():
        rim_wait(pair)
        below_shift = sums_in[line - 1] / float(pixels) - local_mean
        above_shift = sums_in[devices - line - 1] / float(pixels) - local_mean
        inner = 1.0 + beta_lift * (1.0 + 2.0 * alpha_lift)
        for t in range(v1.shape[0]):
            part = slice(t * LANES, (t + 1) * LANES)
            low_half = slice(0, lines // 2)
            next_half = slice(lines, lines + lines // 2)
            fl1[t, low_half] = fl1[t, low_half] + below_shift[:, part] * (1.0 + alpha_lift)
            fl1[t, next_half] = fl1[t, next_half] + below_shift[:, part] * inner
            fr1[t, low_half] = fr1[t, low_half] + above_shift[:, part]
            fr1[t, next_half] = fr1[t, next_half] + above_shift[:, part] * inner
        lift_samples(z1, fl1, fr1, lines, width, first, last, ((v2, 0), (t_ref, 0), (t_ref, one), (t_ref, 2 * one)))
        for t in range(v1.shape[0]):
            v2[t] = v2[t] + shift[:, t * LANES:(t + 1) * LANES]
        state["lines"] = line_copy(1, v2, n2, h, w)
        convert(0, 256)

    def stage_rest():
        closing = line_gather(1, gathers[1])
        stage_b()
        for copy in closing:
            copy.wait()
        for q in range(1, len(rows)):
            place(q, False)

    def stage_b():
        state["lines"].wait()
        lift_lines(v2, n2, z2, h, w, ln)
        rims(z2, h, w, el2, er2)
        state["pair"] = rim_copies(1, el2, er2, fl2, fr2)

    def stage_c():
        rim_wait(state["pair"])
        lift_samples(z2, fl2, fr2, h, w, first, last,
                     ((v3, 0), (t_ref, base2), (t_ref, base2 + two), (t_ref, base2 + 2 * two)))
        state["lines"] = line_copy(2, v3, n3, h // 2, w // 2)

    def stage_d():
        state["lines"].wait()
        lift_lines(v3, n3, z3, h // 2, w // 2, ln)
        rims(z3, h // 2, w // 2, el3, er3)
        state["pair"] = rim_copies(2, el3, er3, fl3, fr3)

    def stage1():
        rim_wait(state["pair"])
        lift_samples(z3, fl3, fr3, h // 2, w // 2, first, last,
                     ((t_ref, base3 + 3 * three), (t_ref, base3), (t_ref, base3 + three), (t_ref, base3 + 2 * three)))
        convert(256 if t_ref.shape[1] > 256 else 0, t_ref.shape[1])

    def pack(dest, at, lane0, wide_out, low_row, count):
        group = LANES // wide_out
        pieces = [rest[pl.ds(low_row + b, count // group, stride=group), :][:, lane0:lane0 + wide_out]
                  for b in range(group)]
        at = at + low_row // group
        dest[at:at + count // group, :] = jnp.concatenate(pieces, axis=1)

    def final(r, first_part, last_part):
        low_row = r * LANES
        count = min(LANES, bands - low_row)
        keep = lax.broadcasted_iota(jnp.int32, (count, LANES), 1) <= lax.broadcasted_iota(jnp.int32, (count, LANES), 0)
        parts = [m[low_row:low_row + count, t * LANES:(t + 1) * LANES] for t in range(r + 1)]
        parts[r] = jnp.where(keep, parts[r], 0.0)
        whole = jnp.concatenate(parts, axis=1)
        upper = whole.astype(jnp.bfloat16)
        lower = (whole - upper.astype(jnp.float32)).astype(jnp.bfloat16)
        left = jnp.concatenate([upper, lower, upper], axis=1)
        chunks = t_ref.shape[1] // LANES
        for q in range(0 if first_part else 2, chunks if last_part else 2, 2):
            pix = slice(q * LANES, min(q + 2, chunks) * LANES)
            big = [th[t, pix, :] for t in range(r + 1)]
            small = [tl[t, pix, :] for t in range(r + 1)]
            right = jnp.concatenate(big + big + small, axis=1)
            out = lax.dot_general(left, right, (((1,), (1,)), ((), ())), preferred_element_type=jnp.float32)
            for b in range(out.shape[1] // LANES):
                part = out[:, b * LANES:(b + 1) * LANES]
                if q + b < o1_ref.shape[0]:
                    o1_ref[q + b, low_row:low_row + count, :] = part
                else:
                    rest[low_row:low_row + count, :] = part
        if not last_part:
            return
        for i in range(3):
            pack(o2_ref, i * (o2_ref.shape[0] // 3), i * two, two, low_row, count)
            pack(o3_ref, i * (o3_ref.shape[0] // 3), 3 * two + i * three, three, low_row, count)
        pack(o4_ref, 0, 3 * two + 3 * three, three, low_row, count)

    stages = {0: stage_a, 1: stage_rest, CSTAGE: stage_c, CSTAGE + 1: stage_d}
    for start in range(0, bands, SUPER):
        superblock(start)
        if start // SUPER in stages:
            stages.pop(start // SUPER)()
    for key in sorted(stages):
        stages[key]()
    for r in range(len(rows)):
        final(r, True, False)
    stage1()
    for r in range(len(rows)):
        final(r, False, True)


def store_kernel(*refs):
    count = len(refs) // 2
    copies = [pltpu.make_async_copy(refs[i], refs[count + i], refs[-1].at[i]) for i in range(count)]
    for copy in copies:
        copy.start()
    for copy in copies:
        copy.wait()


def store_call(arrays):
    return pl.pallas_call(
        store_kernel,
        out_shape=tuple(jax.ShapeDtypeStruct(a.shape, a.dtype) for a in arrays),
        in_specs=[pl.BlockSpec(memory_space=pltpu.VMEM)] * len(arrays),
        out_specs=(pl.BlockSpec(memory_space=pl.ANY),) * len(arrays),
        scratch_shapes=[pltpu.SemaphoreType.DMA((len(arrays),))],
        compiler_params=pltpu.CompilerParams(vmem_limit_bytes=4 * 1024 * 1024),
    )(*arrays)


def gram_call(cube, bands, lines, width):
    pixels = lines * width
    samp, line = lax.axis_size("samp"), lax.axis_size("line")
    devices = samp * line
    rows, offsets = blocks_of(bands)
    used = offsets[-1] + rows[-1]
    unit = 16 * devices
    total = -(-used // unit) * unit
    padded = -(-bands // LANES) * LANES
    f32 = jnp.float32
    sem = pltpu.SemaphoreType.DMA
    return pl.pallas_call(
        functools.partial(gram_kernel, samp, line, bands, lines, width),
        out_shape=(jax.ShapeDtypeStruct((3, bands, LANES), f32),
                   jax.ShapeDtypeStruct((3 * bands * (pixels // 16) // LANES, LANES), f32),
                   jax.ShapeDtypeStruct((3 * bands * (pixels // 64) // LANES, LANES), f32),
                   jax.ShapeDtypeStruct((bands * (pixels // 64) // LANES, LANES), f32)),
        in_specs=[pl.BlockSpec(memory_space=pltpu.VMEM)],
        out_specs=(pl.BlockSpec(memory_space=pltpu.VMEM),) * 4,
        scratch_shapes=[
            pltpu.VMEM((padded // LANES, pixels, LANES), f32),
            pltpu.VMEM((padded // LANES, pixels, LANES), jnp.bfloat16),
            pltpu.VMEM((padded // LANES, pixels, LANES), jnp.bfloat16), pltpu.VMEM((bands, padded), f32),
            pltpu.VMEM((bands, LANES), f32), pltpu.VMEM((total, LANES), f32),
            *[pltpu.VMEM((padded // LANES, pixels // 4 ** i, LANES), f32) for i in (0, 1, 2)],
            *[pltpu.VMEM((padded // LANES, pixels // 4 ** i, LANES), f32) for i in (0, 1, 2)],
            *[pltpu.VMEM((padded // LANES, RIM * width // 2 ** i, LANES), f32) for i in (0, 1, 2)],
            *[pltpu.VMEM((padded // LANES, 2 * lines // 2 ** i, LANES), f32) for i in (0, 0, 1, 1, 2, 2)],
            *[pltpu.VMEM((padded // LANES, 2 * lines // 2 ** i, LANES), f32) for i in (0, 0, 1, 1, 2, 2)],
            sem((3,)), sem((3,)), sem((3, 2)), sem((3, 2)),
            pltpu.VMEM((padded, pixels), f32), pltpu.VMEM((1, padded), f32),
            pltpu.VMEM((devices - 1, 1, padded), f32), pltpu.VMEM((total, LANES), f32),
            pltpu.VMEM((2, line - 1, total // 2 // line, LANES), f32),
            pltpu.VMEM((2, samp - 1, total // 2 // devices, LANES), f32), pltpu.VMEM((total, LANES), f32),
            sem((devices - 1,)), sem((devices - 1,)), sem((2, line - 1)), sem((2, line - 1)),
            sem((2, samp - 1)), sem((2, samp - 1)), sem((2, samp - 1)), sem((2, samp - 1)),
            sem((2, line - 1)), sem((2, line - 1)),
        ],
        compiler_params=pltpu.CompilerParams(collective_id=0, has_side_effects=True,
                                             vmem_limit_bytes=32 * 1024 * 1024),
    )(cube.reshape(-1, LANES))


def local(cube):
    return tuple(out.reshape(-1) for out in store_call(gram_call(cube, BANDS, LD, SD)))


def solution(mesh):
    in_specs = (P(("groups", "samp", "line")),)
    out_specs = (
        P(("groups", "samp", "line")),
        P(("groups", "samp", "line")),
        P(("groups", "samp", "line")),
        P(("groups", "samp", "line")),
    )
    return jax.shard_map(local, mesh=mesh, in_specs=in_specs, out_specs=out_specs, check_vma=False)
```

```python
import functools
import jax
import jax.numpy as jnp
from jax import lax
from jax.experimental import pallas as pl
from jax.experimental.pallas import tpu as pltpu
from jax.sharding import PartitionSpec as P

BANDS = 432
LD = 32
SD = 16

MESH = pl.DeviceIdType.MESH
HIGH = lax.Precision.HIGHEST
LANES = 128
SUPER = 64
CSTAGE = 3


def blocks_of(bands):
    rows = [bands - start for start in range(0, bands, LANES)]
    offsets = [sum(rows[:i]) for i in range(len(rows))]
    return rows, offsets


alpha_lift = -1.586134342059924
beta_lift = -0.052980118572961
gamma_lift = 0.882911075530934
delta_lift = 0.443506852043971
scale_lift = 1.230174104914001
RIM = 4


def lift_list(values):
    evens, odds = values[0::2], values[1::2]
    odds = [o + alpha_lift * (e + f) for o, e, f in zip(odds[:-1], evens[:-1], evens[1:])]
    evens = [e + beta_lift * (o + q) for e, o, q in zip(evens[1:-1], odds[:-1], odds[1:])]
    odds = [o + gamma_lift * (e + f) for o, e, f in zip(odds[1:-1], evens[:-1], evens[1:])]
    evens = [e + delta_lift * (o + q) for e, o, q in zip(evens[1:-1], odds[:-1], odds[1:])]
    return [e * (1.0 / scale_lift) for e in evens], [o * scale_lift for o in odds[1:]]


def lift_lines(src, halo, dst, lines, width, ln, centre=None):
    half = lines // 2
    for t in range(src.shape[0]):
        own = [src[t, i * width:(i + 1) * width] for i in range(lines)]
        got = [halo[t, i * width:(i + 1) * width] for i in range(RIM)]
        if centre is not None:
            middle = centre[:, t * LANES:(t + 1) * LANES]
            own = [o - middle for o in own]
            got = [o - middle for o in got]
        before = [jnp.where(ln == 0, own[RIM - i], got[i]) for i in range(RIM)]
        after = [jnp.where(ln == 0, got[i], own[lines - 2 - i]) for i in range(RIM)]
        low, high = lift_list(before + own + after)
        for i in range(half):
            dst[t, i * width:(i + 1) * width] = low[i]
            dst[t, (half + i) * width:(half + i + 1) * width] = high[i]


def rims(z, lines, width, left, right):
    for t in range(z.shape[0]):
        low = [z[t, pl.ds(s, lines, stride=width), :] for s in range(3)]
        top = [z[t, pl.ds(s, lines, stride=width), :] for s in range(width - 4, width)]
        left[t, :lines] = low[0]
        left[t, lines:] = low[0] + beta_lift * (low[1] + alpha_lift * (low[0] + low[2]))
        right[t, :lines] = top[3] + alpha_lift * top[2]
        right[t, lines:] = top[2] + beta_lift * (top[1] + alpha_lift * (top[0] + top[2]))


def lift_samples(z, from_left, from_right, lines, width, first, last, dests):
    half, n = lines // 2, width // 2
    for t in range(z.shape[0]):
        evens = [z[t, pl.ds(2 * i, lines, stride=width), :] for i in range(n)]
        odds = [z[t, pl.ds(2 * i + 1, lines, stride=width), :] for i in range(n)]
        beyond = jnp.where(last, evens[-1], from_right[t, :lines])
        odds1 = [o + alpha_lift * (e + f) for o, e, f in zip(odds, evens, evens[1:] + [beyond])]
        before = jnp.where(first, odds1[0], from_left[t, :lines] + alpha_lift * evens[0])
        evens1 = [e + beta_lift * (p + o) for e, p, o in zip(evens, [before] + odds1[:-1], odds1)]
        beyond = jnp.where(last, evens1[-1], from_right[t, lines:] + beta_lift * odds1[-1])
        odds2 = [o + gamma_lift * (e + f) for o, e, f in zip(odds1, evens1, evens1[1:] + [beyond])]
        outside = from_left[t, lines:] + beta_lift * before
        before = jnp.where(first, odds2[0], before + gamma_lift * (outside + evens1[0]))
        evens2 = [e + delta_lift * (p + o) for e, p, o in zip(evens1, [before] + odds2[:-1], odds2)]
        for i in range(n):
            low, high = evens2[i] * (1.0 / scale_lift), odds2[i] * scale_lift
            for (ref, base), value in zip(dests, (low[:half], low[half:], high[:half], high[half:])):
                ref[t, pl.ds(base + i, half, stride=n), :] = value


def split3(value):
    first = value.astype(jnp.bfloat16).astype(jnp.float32)
    rest = value - first
    second = rest.astype(jnp.bfloat16).astype(jnp.float32)
    return first, second, rest - second


def gram_kernel(samp, line, bands, lines, width, x_ref, o1_ref, o2_ref, o3_ref, o4_ref, t_ref, th, tl, m, rest, corr, v1, v2, v3, z1, z2, z3, n1, n2, n3, el1, er1, el2, er2, el3, er3, fl1, fr1, fl2, fr2, fl3, fr3,
                l_send, l_recv, r_send, r_recv, xs, sums, sums_in, g, half_in,
                chunk_in, tot, s_send, s_recv, h_send, h_recv, c_send, c_recv, a_send, a_recv,
                b_send, b_recv):
    me, ln = lax.axis_index("samp"), lax.axis_index("line")
    devices = samp * line
    pixels = lines * width
    first, last = me == 0, me == samp - 1
    flat = me * line + ln
    packs = pixels // LANES
    padded = xs.shape[0]

    def peer(d):
        other = lax.rem(flat + d, devices)
        return {"samp": other // line, "line": lax.rem(other, line)}

    def line_copy(level, src, dst, tall, wide):
        rows = RIM * wide
        start = pl.multiple_of((1 - ln) * ((tall - RIM) * wide), 8)
        copy = pltpu.make_async_remote_copy(src.at[:, pl.ds(start, rows)], dst, l_send.at[level], l_recv.at[level],
                                            device_id={"line": 1 - ln}, device_id_type=MESH)
        copy.start()
        return copy

    def rim_copies(level, left, right, from_left, from_right):
        below = pltpu.make_async_remote_copy(left, from_right, r_send.at[level, 0], r_recv.at[level, 0],
                                             device_id={"samp": jnp.maximum(me - 1, 0)}, device_id_type=MESH)
        above = pltpu.make_async_remote_copy(right, from_left, r_send.at[level, 1], r_recv.at[level, 1],
                                             device_id={"samp": jnp.minimum(me + 1, samp - 1)}, device_id_type=MESH)

        @pl.when(me > 0)
        def _():
            below.start()

        @pl.when(me < samp - 1)
        def _():
            above.start()

        return below, above

    def rim_wait(pair):
        below, above = pair

        @pl.when(me > 0)
        def _():
            below.wait_send()
            above.wait_recv()

        @pl.when(me < samp - 1)
        def _():
            above.wait_send()
            below.wait_recv()

    for ref in (fl1, fr1, fl2, fr2, fl3, fr3):
        ref[...] = jnp.zeros_like(ref)
    barrier = pltpu.get_barrier_semaphore()
    for d in range(1, devices):
        pl.semaphore_signal(barrier, inc=1, device_id=peer(d), device_id_type=MESH)
    rows, offsets = blocks_of(bands)
    used = offsets[-1] + rows[-1]
    for q in range(packs):
        part = x_ref[pl.ds(q, bands, stride=packs), :]
        xs[0:bands, q * LANES:(q + 1) * LANES] = part
        if padded > bands:
            xs[bands:, q * LANES:(q + 1) * LANES] = jnp.zeros((padded - bands, LANES), jnp.float32)
    for t in range(v1.shape[0]):
        v1[t] = jnp.transpose(xs[t * LANES:(t + 1) * LANES, :])
    folded = xs[:, 0:LANES]
    for q in range(1, packs):
        folded = folded + xs[:, q * LANES:(q + 1) * LANES]
    folded = jnp.concatenate(split3(folded), axis=1).astype(jnp.bfloat16)
    row_sums = lax.dot_general(jnp.ones((8, 3 * LANES), jnp.bfloat16), folded, (((1,), (1,)), ((), ())),
                               preferred_element_type=jnp.float32)[0:1]
    centre = lax.dot_general(folded, jnp.ones((3 * LANES, LANES), jnp.bfloat16), (((1,), (0,)), ((), ())),
                             preferred_element_type=jnp.float32) / float(pixels)
    parts = [xs[:, q * LANES:(q + 1) * LANES] - centre for q in range(packs)]
    energy = parts[0] * parts[0]
    for part in parts[1:]:
        energy = energy + part * part
    energy = jnp.sum(jnp.sum(energy, axis=0, keepdims=True), axis=1, keepdims=True)
    sum_lane = lax.broadcasted_iota(jnp.int32, (1, padded), 1)
    sums[...] = jnp.where(sum_lane < bands, row_sums, energy)
    local_mean = row_sums / float(pixels)
    coarse = [part.astype(jnp.bfloat16) for part in parts]
    fine = [(part - top_part.astype(jnp.float32)).astype(jnp.bfloat16) for part, top_part in zip(parts, coarse)]
    tall = jnp.concatenate(coarse + coarse + fine + fine, axis=1)
    flat_right = jnp.concatenate(coarse + fine + coarse + fine, axis=1)
    part_rows = g.shape[0] // 2
    half = part_rows // line
    chunk = half // samp

    def line_swap(p):
        made = []
        for d in range(1, line):
            other = lax.rem(ln + d, line)
            copy = pltpu.make_async_remote_copy(
                g.at[pl.ds(pl.multiple_of(p * part_rows + other * half, 8), half)], half_in.at[p, d - 1],
                h_send.at[p, d - 1], h_recv.at[p, d - 1], device_id={"line": other}, device_id_type=MESH)
            copy.start()
            made.append(copy)
        return made

    def scatter(p, swaps):
        for copy in swaps:
            copy.wait()
        mine = pl.ds(pl.multiple_of(p * part_rows + ln * half, 8), half)
        value = g[mine, :]
        for d in range(1, line):
            value = value + half_in[p, d - 1]
        g[mine, :] = value
        made = []
        for d in range(1, samp):
            other = lax.rem(me + d, samp)
            copy = pltpu.make_async_remote_copy(
                g.at[pl.ds(pl.multiple_of(p * part_rows + ln * half + other * chunk, 8), chunk)],
                chunk_in.at[p, d - 1], c_send.at[p, d - 1], c_recv.at[p, d - 1],
                device_id={"samp": other}, device_id_type=MESH)
            copy.start()
            made.append(copy)
        return made

    def gather(p, scatters):
        for copy in scatters:
            copy.wait()
        own = pl.ds(pl.multiple_of(p * part_rows + ln * half + me * chunk, 8), chunk)
        value = g[own, :] + corr[own, :]
        for d in range(1, samp):
            value = value + chunk_in[p, d - 1]
        tot[own, :] = value
        made = []
        for d in range(1, samp):
            other = lax.rem(me + d, samp)
            copy = pltpu.make_async_remote_copy(tot.at[own], tot.at[own], a_send.at[p, d - 1], a_recv.at[p, d - 1],
                                                device_id={"samp": other}, device_id_type=MESH)
            copy.start()
            made.append(copy)
        return made

    def line_gather(p, gathers):
        for copy in gathers:
            copy.wait()
        mine = pl.ds(pl.multiple_of(p * part_rows + ln * half, 8), half)
        made = []
        for d in range(1, line):
            other = lax.rem(ln + d, line)
            copy = pltpu.make_async_remote_copy(tot.at[mine], tot.at[mine], b_send.at[p, d - 1], b_recv.at[p, d - 1],
                                                device_id={"line": other}, device_id_type=MESH)
            copy.start()
            made.append(copy)
        return made

    for q in range(0, len(rows), 2):
        span = min(2 * LANES, padded - q * LANES)
        both = lax.dot_general(tall[q * LANES:bands], flat_right[q * LANES:q * LANES + span],
                               (((1,), (1,)), ((), ())), preferred_element_type=jnp.float32)
        for b in range(span // LANES):
            g[offsets[q + b]:offsets[q + b] + rows[q + b], :] = both[b * LANES:, b * LANES:(b + 1) * LANES]
    if g.shape[0] > used:
        g[used:, :] = jnp.zeros((g.shape[0] - used, LANES), jnp.float32)
    pl.semaphore_wait(barrier, devices - 1)
    copies = []
    for d in range(1, devices):
        copy = pltpu.make_async_remote_copy(sums, sums_in.at[d - 1], s_send.at[d - 1], s_recv.at[d - 1],
                                            device_id=peer(d), device_id_type=MESH)
        copy.start()
        copies.append(copy)
    sum_copies = copies
    swaps = [line_swap(0)]
    lines1 = line_copy(0, v1, n1, lines, width)
    swaps.append(line_swap(1))
    scatters = [scatter(p, swaps[p]) for p in range(2)]
    lines1.wait()
    lift_lines(v1, n1, z1, lines, width, ln, local_mean)
    rims(z1, lines, width, el1, er1)
    for copy in sum_copies:
        copy.wait()
    gathered = jnp.concatenate([sums[...]] + [sums_in[d - 1] for d in range(1, devices)], axis=0)
    all_lane = lax.broadcasted_iota(jnp.int32, (devices, padded), 1)
    traces = jnp.sum(gathered[:, padded - 1:padded], axis=0, keepdims=True)
    means = jnp.where(all_lane < bands, gathered, 0.0) / float(pixels)
    mean = jnp.sum(means, axis=0, keepdims=True) / float(devices)
    spread = means - mean
    trace = traces + float(pixels) * jnp.sum(jnp.sum(spread * spread, axis=0, keepdims=True), axis=1, keepdims=True)
    shift = local_mean - mean
    for q, (count, offset) in enumerate(zip(rows, offsets)):
        corr[offset:offset + count, :] = float(pixels) * lax.dot_general(
            spread[:, q * LANES:], spread[:, q * LANES:(q + 1) * LANES], (((0,), (0,)), ((), ())), precision=HIGH,
            preferred_element_type=jnp.float32)[0:count]
    if g.shape[0] > used:
        corr[used:, :] = jnp.zeros((g.shape[0] - used, LANES), jnp.float32)
    gathers = [gather(0, scatters[0])]
    pair = rim_copies(0, el1, er1, fl1, fr1)
    gathers.append(gather(1, scatters[1]))
    h, w = lines // 2, width // 2
    one = h * w
    two = one // 4
    three = two // 4
    base2, base3 = 3 * one, 3 * one + 3 * two
    closing = line_gather(0, gathers[0])
    for copy in closing:
        copy.wait()
    wide = m.shape[1]
    diag = lax.broadcasted_iota(jnp.int32, (LANES, LANES), 0) == lax.broadcasted_iota(
        jnp.int32, (LANES, LANES), 1)
    scale = 1.0 / float(pixels * devices)
    ridge = trace * scale * (0.01 / bands)

    def place(q, fresh):
        offset = offsets[q]
        for b in range(q, len(rows)):
            size = min(LANES, rows[b])
            start = offset + (b - q) * LANES
            block = tot[start:start + size, :] * scale
            row_part, col_part = slice(q * LANES, q * LANES + size), slice(q * LANES, (q + 1) * LANES)
            if b == q:
                low = jnp.where(diag[:size], block + ridge, block)
                m[row_part, col_part] = low if fresh else m[row_part, col_part] + low
            else:
                if size < LANES:
                    block = jnp.concatenate([block, jnp.zeros((LANES - size, LANES), jnp.float32)], axis=0)
                upper_rows, upper_cols = slice(q * LANES, (q + 1) * LANES), slice(b * LANES, (b + 1) * LANES)
                lower_rows = slice(b * LANES, b * LANES + size)
                flipped = jnp.transpose(block)
                if fresh:
                    m[upper_rows, upper_cols] = flipped
                    m[lower_rows, col_part] = block[:size]
                else:
                    m[upper_rows, upper_cols] = m[upper_rows, upper_cols] + flipped
                    m[lower_rows, col_part] = m[lower_rows, col_part] + block[:size]

    place(0, True)
    m[LANES:, LANES:] = jnp.zeros((bands - LANES, wide - LANES), jnp.float32)
    sub = lax.broadcasted_iota(jnp.int32, (8, LANES), 0)
    lane = lax.broadcasted_iota(jnp.int32, (8, LANES), 1)
    tiles = wide // LANES

    def superblock(start):
        size = min(SUPER, bands - start)
        count = size // 8
        panels = [[m[start + 8 * i:start + 8 * i + 8, t * LANES:(t + 1) * LANES] for t in range(tiles)]
                  for i in range(count)]
        done = []

        def spread(tile, lane0):
            return [jnp.broadcast_to(tile[:, lane0 + e:lane0 + e + 1], (8, LANES)) for e in range(8)]

        ahead = spread(panels[0][start // LANES], start % LANES)
        for k in range(count):
            top = start + 8 * k
            at, lane0 = top // LANES, top % LANES
            own = panels[k]
            cols = ahead
            if k + 1 < count:
                ahead = spread(panels[k + 1][(top + 8) // LANES], (top + 8) % LANES)
            later = range(k + 1, count)
            below = {p: [jnp.broadcast_to(panels[p][at][:, lane0 + e:lane0 + e + 1], (8, LANES)) for e in range(8)]
                     for p in later}
            inside = (lane >= lane0) & (lane < lane0 + 8)
            own[at] = jnp.where(inside, jnp.where(lane - lane0 == sub, 1.0, 0.0), own[at])
            for p in later:
                panels[p][at] = jnp.where(inside, 0.0, panels[p][at])
            pivots = None
            for b in range(8):
                pivot = jnp.broadcast_to(cols[b][b:b + 1, :], (8, LANES))
                inverse = 1.0 / pivot
                pivots = pivot if pivots is None else jnp.where(sub == b, pivot, pivots)
                factor = jnp.where(sub > b, cols[b] * inverse, 0.0)
                rows_b = [jnp.broadcast_to(own[t][b:b + 1, :], (8, LANES)) for t in range(tiles)]
                heads = {e: jnp.broadcast_to(cols[e][b:b + 1, :], (8, LANES)) for e in range(b + 1, 8)}
                for e in range(b + 1, 8):
                    cols[e] = cols[e] - factor * heads[e]
                for p in later:
                    scaled = below[p][b] * inverse
                    if p == k + 1:
                        ahead = [ahead[e] - scaled * jnp.broadcast_to(below[p][b][e:e + 1, :], (8, LANES))
                                 for e in range(8)]
                    for e in range(b + 1, 8):
                        below[p][e] = below[p][e] - scaled * heads[e]
                    for t in range(tiles):
                        panels[p][t] = panels[p][t] - scaled * rows_b[t]
                if b < 7:
                    for t in range(tiles):
                        own[t] = own[t] - factor * rows_b[t]
            root = lax.rsqrt(pivots)
            done.append([own[t] * root for t in range(tiles)])
            for t in range(tiles):
                m[top:top + 8, t * LANES:(t + 1) * LANES] = done[k][t]
        below_at = start + size
        if below_at >= bands:
            return
        full = [jnp.concatenate([done[k][t] for k in range(count)], axis=0) for t in range(tiles)]
        kept = list(full)
        row_ids = lax.broadcasted_iota(jnp.int32, (size, LANES), 0) + start % LANES
        lane_ids = lax.broadcasted_iota(jnp.int32, (size, LANES), 1)
        upper = (lane_ids > row_ids) & (lane_ids < start % LANES + size)
        kept[start // LANES] = jnp.where(upper, 0.0, kept[start // LANES])
        splits = [split3(part) for part in kept]
        terms = ((0, 0), (1, 0), (2, 0), (0, 1), (0, 2), (1, 1))
        copies = LANES // size
        depth = -(-len(terms) // copies)
        zero = jnp.zeros((size, LANES), jnp.float32)
        right = jnp.concatenate(
            [jnp.concatenate([splits[t][b] for a, b in terms] + [zero] * (depth * copies - len(terms)), axis=0)
             for t in range(tiles)], axis=1).astype(jnp.bfloat16)
        which = lax.broadcasted_iota(jnp.int32, (LANES, LANES), 1) // size
        for t in range(below_at // LANES, tiles):
            flipped = split3(jnp.transpose(jnp.concatenate([full[t]] * copies, axis=0)))
            pieces = []
            for g in range(depth):
                group = [flipped[a] for a, b in terms[g * copies:(g + 1) * copies]]
                piece = group[0]
                for i in range(1, copies):
                    piece = jnp.where(which == i, group[i] if i < len(group) else 0.0, piece)
                pieces.append(piece)
            left = jnp.concatenate(pieces, axis=1).astype(jnp.bfloat16)
            lo = max(below_at, t * LANES)
            bounds = [lo]
            while bounds[-1] < min(bands, (t + 1) * LANES):
                bounds.append(min(bounds[-1] + SUPER, bands, (t + 1) * LANES))
            for low_row, high_row in zip(bounds[:-1], bounds[1:]):
                update = lax.dot_general(
                    left[low_row - t * LANES:high_row - t * LANES], right, (((1,), (0,)), ((), ())),
                    preferred_element_type=jnp.float32)
                for u in range(tiles):
                    old = m[low_row:high_row, u * LANES:(u + 1) * LANES]
                    if start // LANES == u:
                        lanes = lax.broadcasted_iota(jnp.int32, (high_row - low_row, LANES), 1)
                        old = jnp.where((lanes >= start % LANES) & (lanes < start % LANES + size), 0.0, old)
                    m[low_row:high_row, u * LANES:(u + 1) * LANES] = old - update[:, u * LANES:(u + 1) * LANES]

    state = {}

    def convert(low_pix, high_pix):
        for t in range(tiles):
            top_part = t_ref[t, low_pix:high_pix].astype(jnp.bfloat16)
            th[t, low_pix:high_pix] = top_part
            tl[t, low_pix:high_pix] = (t_ref[t, low_pix:high_pix] - top_part.astype(jnp.float32)).astype(jnp.bfloat16)

    def stage_a():
        rim_wait(pair)
        below_shift = sums_in[line - 1] / float(pixels) - local_mean
        above_shift = sums_in[devices - line - 1] / float(pixels) - local_mean
        inner = 1.0 + beta_lift * (1.0 + 2.0 * alpha_lift)
        for t in range(v1.shape[0]):
            part = slice(t * LANES, (t + 1) * LANES)
            low_half = slice(0, lines // 2)
            next_half = slice(lines, lines + lines // 2)
            fl1[t, low_half] = fl1[t, low_half] + below_shift[:, part] * (1.0 + alpha_lift)
            fl1[t, next_half] = fl1[t, next_half] + below_shift[:, part] * inner
            fr1[t, low_half] = fr1[t, low_half] + above_shift[:, part]
            fr1[t, next_half] = fr1[t, next_half] + above_shift[:, part] * inner
        lift_samples(z1, fl1, fr1, lines, width, first, last, ((v2, 0), (t_ref, 0), (t_ref, one), (t_ref, 2 * one)))
        for t in range(v1.shape[0]):
            v2[t] = v2[t] + shift[:, t * LANES:(t + 1) * LANES]
        state["lines"] = line_copy(1, v2, n2, h, w)
        convert(0, 256)

    def stage_rest():
        closing = line_gather(1, gathers[1])
        stage_b()
        for copy in closing:
            copy.wait()
        for q in range(1, len(rows)):
            place(q, False)

    def stage_b():
        state["lines"].wait()
        lift_lines(v2, n2, z2, h, w, ln)
        rims(z2, h, w, el2, er2)
        state["pair"] = rim_copies(1, el2, er2, fl2, fr2)

    def stage_c():
        rim_wait(state["pair"])
        lift_samples(z2, fl2, fr2, h, w, first, last,
                     ((v3, 0), (t_ref, base2), (t_ref, base2 + two), (t_ref, base2 + 2 * two)))
        state["lines"] = line_copy(2, v3, n3, h // 2, w // 2)

    def stage_d():
        state["lines"].wait()
        lift_lines(v3, n3, z3, h // 2, w // 2, ln)
        rims(z3, h // 2, w // 2, el3, er3)
        state["pair"] = rim_copies(2, el3, er3, fl3, fr3)

    def stage1():
        rim_wait(state["pair"])
        lift_samples(z3, fl3, fr3, h // 2, w // 2, first, last,
                     ((t_ref, base3 + 3 * three), (t_ref, base3), (t_ref, base3 + three), (t_ref, base3 + 2 * three)))
        convert(256 if t_ref.shape[1] > 256 else 0, t_ref.shape[1])

    def pack(dest, at, lane0, wide_out, low_row, count):
        group = LANES // wide_out
        pieces = [rest[pl.ds(low_row + b, count // group, stride=group), :][:, lane0:lane0 + wide_out]
                  for b in range(group)]
        at = at + low_row // group
        dest[at:at + count // group, :] = jnp.concatenate(pieces, axis=1)

    def final(r, first_part, last_part):
        low_row = r * LANES
        count = min(LANES, bands - low_row)
        keep = lax.broadcasted_iota(jnp.int32, (count, LANES), 1) <= lax.broadcasted_iota(jnp.int32, (count, LANES), 0)
        parts = [m[low_row:low_row + count, t * LANES:(t + 1) * LANES] for t in range(r + 1)]
        parts[r] = jnp.where(keep, parts[r], 0.0)
        whole = jnp.concatenate(parts, axis=1)
        upper = whole.astype(jnp.bfloat16)
        lower = (whole - upper.astype(jnp.float32)).astype(jnp.bfloat16)
        left = jnp.concatenate([upper, lower, upper], axis=1)
        chunks = t_ref.shape[1] // LANES
        for q in range(0 if first_part else 2, chunks if last_part else 2, 2):
            pix = slice(q * LANES, min(q + 2, chunks) * LANES)
            big = [th[t, pix, :] for t in range(r + 1)]
            small = [tl[t, pix, :] for t in range(r + 1)]
            right = jnp.concatenate(big + big + small, axis=1)
            out = lax.dot_general(left, right, (((1,), (1,)), ((), ())), preferred_element_type=jnp.float32)
            for b in range(out.shape[1] // LANES):
                part = out[:, b * LANES:(b + 1) * LANES]
                if q + b < o1_ref.shape[0]:
                    o1_ref[q + b, low_row:low_row + count, :] = part
                else:
                    rest[low_row:low_row + count, :] = part
        if not last_part:
            return
        for i in range(3):
            pack(o2_ref, i * (o2_ref.shape[0] // 3), i * two, two, low_row, count)
            pack(o3_ref, i * (o3_ref.shape[0] // 3), 3 * two + i * three, three, low_row, count)
        pack(o4_ref, 0, 3 * two + 3 * three, three, low_row, count)

    stages = {0: stage_a, 1: stage_rest, CSTAGE: stage_c, CSTAGE + 1: stage_d}
    for start in range(0, bands, SUPER):
        superblock(start)
        if start // SUPER in stages:
            stages.pop(start // SUPER)()
    for key in sorted(stages):
        stages[key]()
    for r in range(len(rows)):
        final(r, True, False)
    stage1()
    for r in range(len(rows)):
        final(r, False, True)


def store_kernel(*refs):
    count = len(refs) // 2
    copies = [pltpu.make_async_copy(refs[i], refs[count + i], refs[-1].at[i]) for i in range(count)]
    for copy in copies:
        copy.start()
    for copy in copies:
        copy.wait()


def store_call(arrays):
    return pl.pallas_call(
        store_kernel,
        out_shape=tuple(jax.ShapeDtypeStruct(a.shape, a.dtype) for a in arrays),
        in_specs=[pl.BlockSpec(memory_space=pltpu.VMEM)] * len(arrays),
        out_specs=(pl.BlockSpec(memory_space=pl.ANY),) * len(arrays),
        scratch_shapes=[pltpu.SemaphoreType.DMA((len(arrays),))],
        compiler_params=pltpu.CompilerParams(vmem_limit_bytes=4 * 1024 * 1024),
    )(*arrays)


def gram_call(cube, bands, lines, width):
    pixels = lines * width
    samp, line = lax.axis_size("samp"), lax.axis_size("line")
    devices = samp * line
    rows, offsets = blocks_of(bands)
    used = offsets[-1] + rows[-1]
    unit = 16 * devices
    total = -(-used // unit) * unit
    padded = -(-bands // LANES) * LANES
    f32 = jnp.float32
    sem = pltpu.SemaphoreType.DMA
    return pl.pallas_call(
        functools.partial(gram_kernel, samp, line, bands, lines, width),
        out_shape=(jax.ShapeDtypeStruct((3, bands, LANES), f32),
                   jax.ShapeDtypeStruct((3 * bands * (pixels // 16) // LANES, LANES), f32),
                   jax.ShapeDtypeStruct((3 * bands * (pixels // 64) // LANES, LANES), f32),
                   jax.ShapeDtypeStruct((bands * (pixels // 64) // LANES, LANES), f32)),
        in_specs=[pl.BlockSpec(memory_space=pltpu.VMEM)],
        out_specs=(pl.BlockSpec(memory_space=pltpu.VMEM),) * 4,
        scratch_shapes=[
            pltpu.VMEM((padded // LANES, pixels, LANES), f32),
            pltpu.VMEM((padded // LANES, pixels, LANES), jnp.bfloat16),
            pltpu.VMEM((padded // LANES, pixels, LANES), jnp.bfloat16), pltpu.VMEM((bands, padded), f32),
            pltpu.VMEM((bands, LANES), f32), pltpu.VMEM((total, LANES), f32),
            *[pltpu.VMEM((padded // LANES, pixels // 4 ** i, LANES), f32) for i in (0, 1, 2)],
            *[pltpu.VMEM((padded // LANES, pixels // 4 ** i, LANES), f32) for i in (0, 1, 2)],
            *[pltpu.VMEM((padded // LANES, RIM * width // 2 ** i, LANES), f32) for i in (0, 1, 2)],
            *[pltpu.VMEM((padded // LANES, 2 * lines // 2 ** i, LANES), f32) for i in (0, 0, 1, 1, 2, 2)],
            *[pltpu.VMEM((padded // LANES, 2 * lines // 2 ** i, LANES), f32) for i in (0, 0, 1, 1, 2, 2)],
            sem((3,)), sem((3,)), sem((3, 2)), sem((3, 2)),
            pltpu.VMEM((padded, pixels), f32), pltpu.VMEM((1, padded), f32),
            pltpu.VMEM((devices - 1, 1, padded), f32), pltpu.VMEM((total, LANES), f32),
            pltpu.VMEM((2, line - 1, total // 2 // line, LANES), f32),
            pltpu.VMEM((2, samp - 1, total // 2 // devices, LANES), f32), pltpu.VMEM((total, LANES), f32),
            sem((devices - 1,)), sem((devices - 1,)), sem((2, line - 1)), sem((2, line - 1)),
            sem((2, samp - 1)), sem((2, samp - 1)), sem((2, samp - 1)), sem((2, samp - 1)),
            sem((2, line - 1)), sem((2, line - 1)),
        ],
        compiler_params=pltpu.CompilerParams(collective_id=0, has_side_effects=True,
                                             vmem_limit_bytes=32 * 1024 * 1024),
    )(cube.reshape(-1, LANES))


def local(cube):
    return tuple(out.reshape(-1) for out in store_call(gram_call(cube, BANDS, LD, SD)))


def solution(mesh):
    in_specs = (P(("groups", "samp", "line")),)
    out_specs = (
        P(("groups", "samp", "line")),
        P(("groups", "samp", "line")),
        P(("groups", "samp", "line")),
        P(("groups", "samp", "line")),
    )
    return jax.shard_map(local, mesh=mesh, in_specs=in_specs, out_specs=out_specs, check_vma=False)
```
